256 devices in a mesh: seq: 128 (over z, x, y_hi, core), dp: 2 (over y_lo).
Axes of the slice: x: 4, y: 4 (y_hi: 2, y_lo: 2; y = y_hi * 2 + y_lo), z: 8, core: 2. Of those that a mesh axis runs over, the one named last changes fastest.
Arguments:
- features: bfloat16 [2, 32768, 2048], P('dp', 'seq'), may hold values from -24 to 24
- queries: bfloat16 [2, 32768, 1024], P('dp', 'seq'), may hold values from -136 to 136
- kv_weight: bfloat16 [2048, 2048], P('dp'), may hold values from -0.125 to 0.125
- upstream: bfloat16 [2, 32768, 1024], P('dp', 'seq'), may hold values from -6 to 6
Outputs:
- attended: bfloat16 [2, 32768, 1024], P('dp', 'seq')
- query_grad: bfloat16 [2, 32768, 1024], P('dp', 'seq')
- feature_grad: bfloat16 [2, 32768, 2048], P('dp', 'seq')
- weight_grad: float32 [2048, 2048], P(('dp', 'seq'))
The draws below stay inside these ranges and needn't reach their ends.
All inputs are finite; a program needn't handle non-finite values.
Results may differ from the reference program's by a relative error of at most 0.013.
The reference program's roundings to bfloat16 on the way (of `own_kv`, `weights`, `dscore` and `kv_grad`) count: a program that leaves them out, or rounds other values in their place, can miss the bound.
Values may be sent and summed in bfloat16 or wider, within the bound.
A program may use at most 128 MiB of HBM per device.

```python
import math
import jax
import jax.numpy as jnp
from jax import lax

D = 2048
HEADS = 8
HEAD_DIM = 128
WINDOW = 2048
TOK_DEV = 256
HW = 1024
TOKENS = 32768
SAMPLES = 2
N_SEQ = 128


def draw_queries(key, part):
    value_key = jax.random.fold_in(key, 21)
    shape = (SAMPLES, TOKENS, HEADS * HEAD_DIM)
    return jnp.clip(jax.random.normal(value_key, shape, jnp.float32), -5.0, 5.0).astype(jnp.bfloat16)


def draw_upstream(key, part):
    value_key = jax.random.fold_in(key, 31)
    shape = (SAMPLES, TOKENS, HEADS * HEAD_DIM)
    return jnp.clip(jax.random.normal(value_key, shape, jnp.float32), -6.0, 6.0).astype(jnp.bfloat16)


def spiked(entries, stream_key, source, target, parts, factor):
    owner, partner = [(jnp.arange(entries.shape[dim]) // (entries.shape[dim] // parts)).reshape([-1 if axis == dim else 1 for axis in range(entries.ndim)]) for dim in (source, target)]
    chosen = jax.random.permutation(stream_key, parts)[partner]
    strong = (owner == chosen) | (owner == (partner + parts // 2) % parts)
    return jnp.where(strong, factor * entries, entries)


def block_levels(stream_key, extent, pieces, least, high):
    loudness, own = 1.0, jax.random.fold_in(stream_key, 6)
    for position, shards_of in pieces:
        draws = jnp.exp(jax.random.uniform(jax.random.fold_in(own, position), (shards_of,), jnp.float32, least / len(pieces), high / len(pieces)))
        loudness = loudness * jnp.repeat(draws, extent[position] // shards_of).reshape([-1 if axis == position else 1 for axis in range(len(extent))])
    return loudness


def noise(stream_key, extent, deviation, reach, shards=(), kind=jnp.bfloat16):
    result = deviation * jax.random.normal(stream_key, extent, jnp.float32)
    if shards:
        result = result * block_levels(stream_key, extent, shards, -0.22, 0.18)
    return jnp.clip(result, -reach, reach).astype(kind)


def bell_draw_with(own_key, dims, width, bound, split, heavy, kind=jnp.bfloat16):
    entries = width * jax.random.normal(own_key, dims, jnp.float32)
    if split:
        entries = entries * block_levels(own_key, dims, split, -0.22, 0.18)
    return jnp.clip(spiked(entries, jax.random.fold_in(own_key, 3), *heavy), -bound, bound).astype(kind)


def setup_inputs(seed: int = 0) -> dict:
    streams_of = jax.random.split(jax.random.key(seed), 5)
    return {
        "features": bell_draw_with(streams_of[0], (SAMPLES, TOKENS, D), 1.0, 24.0, ((0, 2), (1, 128)), (1, 2, 128, 5.5)),
        "queries": draw_queries(jax.random.fold_in(streams_of[4], 71), 0),
        "kv_weight": noise(streams_of[2], (D, 2 * HW), D ** -0.5, 0.125, ((0, 2),)),
        "upstream": draw_upstream(jax.random.fold_in(streams_of[4], 71), 0),
    }


def attend_block(query_rows, upstream_rows, window_kv, block_index):
    span = WINDOW // TOK_DEV
    key_count = (span + 1) * TOK_DEV
    head_width = HEADS * HEAD_DIM
    score_scale = 1.0 / math.sqrt(HEAD_DIM)
    query_heads = query_rows.astype(jnp.float32).reshape(TOK_DEV, HEADS, HEAD_DIM)
    grad_heads = upstream_rows.astype(jnp.float32).reshape(TOK_DEV, HEADS, HEAD_DIM)
    key_heads = window_kv[:, :head_width].astype(jnp.float32).reshape(key_count, HEADS, HEAD_DIM)
    value_heads = window_kv[:, head_width:].astype(jnp.float32).reshape(key_count, HEADS, HEAD_DIM)
    query_pos = lax.broadcasted_iota(jnp.int32, (TOK_DEV, key_count), 0)
    key_pos = lax.broadcasted_iota(jnp.int32, (TOK_DEV, key_count), 1) - span * TOK_DEV
    first_pos = block_index.astype(jnp.int32) * TOK_DEV
    allowed = (key_pos <= query_pos) & (key_pos > query_pos - WINDOW) & (first_pos + key_pos >= 0)
    scores = jnp.einsum('ihd,jhd->hij', query_heads, key_heads) * score_scale
    scores = jnp.where(allowed[None], scores, -1e+30)
    row_max = lax.optimization_barrier(jnp.max(scores, axis=-1, keepdims=True))
    exp_scores = jnp.exp(scores - row_max)
    probability = exp_scores / lax.optimization_barrier(jnp.sum(exp_scores, axis=-1, keepdims=True))
    weights = probability.astype(jnp.bfloat16)
    weights_wide = lax.optimization_barrier(weights).astype(jnp.float32)
    attended = jnp.einsum('hij,jhd->ihd', weights_wide, value_heads).astype(jnp.bfloat16)
    dprob = jnp.einsum('ihd,jhd->hij', grad_heads, value_heads)
    centred = dprob - lax.optimization_barrier(jnp.sum(probability * dprob, axis=-1, keepdims=True))
    dscore = lax.optimization_barrier((probability * centred * score_scale).astype(jnp.bfloat16)).astype(jnp.float32)
    query_grad = jnp.einsum('hij,jhd->ihd', dscore, key_heads).astype(jnp.bfloat16)
    key_grad = jnp.einsum('hij,ihd->jhd', dscore, query_heads)
    value_grad = jnp.einsum('hij,ihd->jhd', weights_wide, grad_heads)
    kv_grad_all = jnp.concatenate([key_grad.reshape(key_count, head_width), value_grad.reshape(key_count, head_width)], axis=1)
    return (attended.reshape(TOK_DEV, head_width), query_grad.reshape(TOK_DEV, head_width), kv_grad_all)

def one_sample(item):
    own_kv, query_rows, upstream_rows = item
    span = WINDOW // TOK_DEV
    head_width = HEADS * HEAD_DIM
    padded = jnp.concatenate([jnp.zeros((span, TOK_DEV, 2 * head_width), jnp.bfloat16), own_kv], axis=0)
    zero_index = jnp.zeros((), jnp.int32)

    def visit(pending, inputs):
        query_block, upstream_block, block_index = inputs
        window_kv = lax.dynamic_slice(padded, (block_index.astype(jnp.int32), zero_index, zero_index), (span + 1, TOK_DEV, 2 * head_width))
        window_kv = window_kv.reshape((span + 1) * TOK_DEV, 2 * head_width)
        attended, query_grad, kv_grad_all = attend_block(query_block, upstream_block, window_kv, block_index)
        kv_grad_all = kv_grad_all.reshape(span + 1, TOK_DEV, 2 * head_width)
        own_total = kv_grad_all[span] + pending[0]
        remote = lax.optimization_barrier(kv_grad_all[:span].astype(jnp.bfloat16)).astype(jnp.float32)[::-1]
        shifted = jnp.concatenate([pending[1:], jnp.zeros((1, TOK_DEV, 2 * head_width), jnp.float32)], axis=0)
        return (shifted + remote, (attended, query_grad, own_total.astype(jnp.bfloat16)))
    start = jnp.zeros((span, TOK_DEV, 2 * head_width), jnp.float32)
    block_ids = jnp.arange(N_SEQ, dtype=jnp.int32)
    final, outputs = lax.scan(visit, start, (query_rows, upstream_rows, block_ids), reverse=True)
    return outputs

def reference(features, queries, kv_weight, upstream):
    head_width = HEADS * HEAD_DIM
    flat = features.reshape(SAMPLES * TOKENS, D)
    own_kv = jnp.dot(flat, kv_weight, preferred_element_type=jnp.float32).astype(jnp.bfloat16)
    own_kv = own_kv.reshape(SAMPLES, N_SEQ, TOK_DEV, 2 * head_width)
    query_rows = queries.reshape(SAMPLES, N_SEQ, TOK_DEV, head_width)
    upstream_rows = upstream.reshape(SAMPLES, N_SEQ, TOK_DEV, head_width)
    attended, query_grad, kv_grad = lax.map(one_sample, (own_kv, query_rows, upstream_rows))
    kv_grad = kv_grad.reshape(SAMPLES * TOKENS, 2 * head_width)
    feature_grad = lax.dot_general(kv_grad, kv_weight, (((1,), (1,)), ((), ())), preferred_element_type=jnp.float32)
    feature_grad = feature_grad.astype(jnp.bfloat16).reshape(SAMPLES, TOKENS, D)
    weight_grad = lax.dot_general(flat, kv_grad, (((0,), (0,)), ((), ())), preferred_element_type=jnp.float32)
    return (attended.reshape(SAMPLES, TOKENS, head_width), query_grad.reshape(SAMPLES, TOKENS, head_width), feature_grad, weight_grad)
```

```python
import math

import jax
import jax.numpy as jnp
from jax import lax
from jax.experimental import pallas as pl
from jax.experimental.pallas import tpu as pltpu
from jax.sharding import PartitionSpec as P

HD = 128
BLK = 256
SPAN = 8
NEG = -1e30
MESH = pl.DeviceIdType.MESH
BF = jnp.bfloat16
F32 = jnp.float32
SCALE = 1.0 / math.sqrt(HD)
EXP_SCALE = SCALE * math.log2(math.e)
NT = (((1,), (1,)), ((), ()))
TN = (((0,), (0,)), ((), ()))


def loop(lo, hi, body):
    def step(i, carry):
        body(i)
        return carry

    lax.fori_loop(lo, hi, step, 0)


def place():
    seq = lax.axis_index("seq")
    dp = lax.axis_index("dp")
    return seq, dp, seq % 4, seq - seq % 4


def remote(src, dst, send, recv, seq, dp):
    return pltpu.make_async_remote_copy(
        src_ref=src, dst_ref=dst, send_sem=send, recv_sem=recv,
        device_id={"seq": seq, "dp": dp}, device_id_type=MESH,
    )


def greet(partners):
    barrier = pltpu.get_barrier_semaphore()
    for seq, dp in partners:
        pl.semaphore_signal(barrier, inc=1, device_id={"seq": seq, "dp": dp}, device_id_type=MESH)
    pl.semaphore_wait(barrier, len(partners))


def attention_kernel(
    x_in, q_in, w_in, up_in,
    att_out, dq_out, fg_out, kvf_out, fall_out,
    wf, xv, stage, kbuf, kvt, qbuf, s_ref, dp_ref, dkv, sbuf, rbuf, kvf, kvg, obuf, fgv,
    wl, ws, wr, wfs, wfr, xl, ks, kr, kl, hs, hr, qs, qr, ql, fs, fr, fl,
    os_, or_, ol, rs, rr, gs, gr, gl, el,
):
    n_seq = lax.axis_size("seq")
    seq, dp, me, base = place()
    core = seq % 2
    y_hi = (seq // 2) % 2
    other = 1 - dp
    up_y = (y_hi + dp) % 2
    down_y = (y_hi + 1 - dp) % 2
    up_seq = base + up_y * 2 + core
    down_seq = base + down_y * 2 + core
    w_seq = base + ((y_hi + (1 - dp) * (1 - core) + dp * core) % 2) * 2 + core
    pair_seq = base + y_hi * 2 + (1 - core)
    near_next = (seq + 4) % n_seq
    far_next = (seq + 8) % n_seq
    near_prev = (seq + n_seq - 4) % n_seq
    far_prev = (seq + n_seq - 8) % n_seq

    def cols(head_pos, kv):
        return pl.ds(pl.multiple_of(kv * 1024 + head_pos * HD, HD), HD)

    def w_local(hl, j, kv):
        return pltpu.make_async_copy(
            w_in.at[:, cols(2 * j + hl, kv)],
            wf.at[hl * 4 + j, pl.ds(pl.multiple_of(dp * 1024, 1024), 1024), pl.ds(kv * HD, HD)],
            wl.at[hl * 4 + j, kv],
        )

    def w_rows(which_dp, which_core):
        return pl.ds(pl.multiple_of(which_dp * 1024 + which_core * 512, 512), 512)

    def w_send(hl, j, kv):
        return remote(
            w_in.at[pl.ds(pl.multiple_of(core * 512, 512), 512), cols(2 * j + hl, kv)],
            wf.at[hl * 4 + j, w_rows(dp, core), pl.ds(kv * HD, HD)],
            ws.at[hl * 4 + j, kv], wr.at[hl * 4 + j, kv], w_seq, other,
        )

    def w_arrive(hl, j, kv):
        part = wf.at[hl * 4 + j, w_rows(other, core), pl.ds(kv * HD, HD)]
        return remote(part, part, ws.at[hl * 4 + j, kv], wr.at[hl * 4 + j, kv], w_seq, other)

    def w_swap(hl, j, which_core):
        part = wf.at[hl * 4 + j, w_rows(other, which_core), :]
        return remote(part, part, wfs.at[hl * 4 + j], wfr.at[hl * 4 + j], pair_seq, dp)

    def kv_send(hl, j):
        return remote(
            stage.at[hl * 4 + j], kbuf.at[hl, SPAN + me], ks.at[hl, j], kr.at[hl, me], base + j, dp
        )

    def kv_arrive(hl, j):
        return remote(
            stage.at[hl * 4 + j], kbuf.at[hl, SPAN + j], ks.at[hl, j], kr.at[hl, j], base + j, dp
        )

    def kv_local(hl):
        return pltpu.make_async_copy(stage.at[hl * 4 + me], kbuf.at[hl, SPAN + me], kl.at[hl])

    def halo(hl, i, far):
        return remote(
            kbuf.at[hl, SPAN + i], kbuf.at[hl, (1 - far) * 4 + i],
            hs.at[hl, far, i], hr.at[hl, far, i], far_next if far else near_next, dp,
        )

    def q_copy(hl, j, which):
        src = (q_in, up_in)[which].at[:, cols(2 * j + hl, 0)]
        return src, qbuf.at[hl, me, :, pl.ds(which * HD, HD)]

    def q_send(hl, j, which):
        src, dst = q_copy(hl, j, which)
        return remote(src, dst, qs.at[hl, j, which], qr.at[hl, me, which], base + j, dp)

    def q_arrive(hl, j, which):
        src, _ = q_copy(hl, j, which)
        return remote(
            src, qbuf.at[hl, j, :, pl.ds(which * HD, HD)],
            qs.at[hl, j, which], qr.at[hl, j, which], base + j, dp,
        )

    def q_local(hl, which):
        src, dst = q_copy(hl, me, which)
        return pltpu.make_async_copy(src, dst, ql.at[hl, which])

    def x_cols(which_dp):
        return x_in.at[:, pl.ds(pl.multiple_of(which_dp * 1024, 1024), 1024)]

    def f_send(j, d):
        return remote(x_cols(d), fall_out.at[dp, me], fs.at[d, j], fr.at[dp, me], base + j, d)

    def f_arrive(j, d):
        return remote(x_cols(d), fall_out.at[d, j], fs.at[d, j], fr.at[d, j], base + j, d)

    def f_local():
        return pltpu.make_async_copy(x_cols(dp), fall_out.at[dp, me], fl)

    def o_send(hl, j, which):
        out = (att_out, dq_out)[which]
        return remote(
            obuf.at[hl, j, :, pl.ds(which * HD, HD)], out.at[:, cols(2 * me + hl, 0)],
            os_.at[hl, j, which], or_.at[hl, me, which], base + j, dp,
        )

    def o_arrive(hl, j, which):
        out = (att_out, dq_out)[which]
        return remote(
            obuf.at[hl, j, :, pl.ds(which * HD, HD)], out.at[:, cols(2 * j + hl, 0)],
            os_.at[hl, j, which], or_.at[hl, j, which], base + j, dp,
        )

    def o_local(hl, which):
        out = (att_out, dq_out)[which]
        return pltpu.make_async_copy(
            obuf.at[hl, me, :, pl.ds(which * HD, HD)], out.at[:, cols(2 * me + hl, 0)],
            ol.at[hl, which],
        )

    def back(hl, i, far):
        return remote(
            sbuf.at[hl, (1 - far) * 4 + i], rbuf.at[hl, far, i],
            rs.at[hl, far, i], rr.at[hl, far, i], far_prev if far else near_prev, dp,
        )

    def g_send(hl, j):
        return remote(
            kvf.at[hl, j], kvg.at[hl * 4 + me], gs.at[hl, j], gr.at[hl, me], base + j, dp
        )

    def g_arrive(hl, j):
        return remote(
            kvf.at[hl, j], kvg.at[hl * 4 + j], gs.at[hl, j], gr.at[hl, j], base + j, dp
        )

    def g_local(hl):
        return pltpu.make_async_copy(kvf.at[hl, me], kvg.at[hl * 4 + me], gl.at[hl])

    def others(body):
        loop(1, 4, lambda r: body((me + r) % 4))

    def project(hl):
        def forward(j):
            w_arrive(hl, j, 0).wait_recv()
            w_arrive(hl, j, 1).wait_recv()
            w_swap(hl, j, core).start()

        loop(0, 4, forward)

        def one(r):
            j = (me + r) % 4
            w_local(hl, j, 0).wait()
            w_local(hl, j, 1).wait()
            w_swap(hl, j, 1 - core).wait_recv()
            kv = jnp.dot(xv[...], wf[hl * 4 + j], preferred_element_type=F32)
            stage[hl * 4 + j] = kv.astype(BF)

            @pl.when(r < 4)
            def _():
                kv_send(hl, j).start()

            @pl.when(r == 4)
            def _():
                kv_local(hl).start()

        loop(1, 5, one)

    def send_halo(hl):
        kv_local(hl).wait()

        def go(i):
            halo(hl, i, 0).start()
            halo(hl, i, 1).start()

        go(me)

        def one(i):
            kv_arrive(hl, i).wait_recv()
            go(i)

        others(one)

    def attend(hl):
        def clear(b):
            dkv[hl, b] = jnp.zeros((BLK, 2 * HD), F32)
            kvt[b] = kbuf[hl, b].T

        loop(0, 12, clear)
        rows = lax.broadcasted_iota(jnp.int32, (BLK, BLK), 0)
        columns = lax.broadcasted_iota(jnp.int32, (BLK, BLK), 1)

        def one_block(qi):
            query = qbuf[hl, qi, :, :HD]
            grad = qbuf[hl, qi, :, HD:]
            first = base - SPAN + qi
            top = None
            for w in range(SPAN + 1):
                scores = lax.dot_general(
                    kbuf[hl, qi + w, :, :HD], query, NT, preferred_element_type=F32
                )
                if w == 0:
                    scores = jnp.where(rows > columns, scores, NEG)
                if w == SPAN:
                    scores = jnp.where(rows <= columns, scores, NEG)
                s_ref[w] = scores
                here = jnp.max(scores, axis=0, keepdims=True)
                if w < SPAN:
                    here = jnp.where(first + w >= 0, here, NEG)
                top = here if top is None else jnp.maximum(top, here)
                dp_ref[w] = lax.dot_general(
                    kbuf[hl, qi + w, :, HD:], grad, NT, preferred_element_type=F32
                )
            top = top * EXP_SCALE
            total = jnp.zeros((1, BLK), F32)
            weighted = jnp.zeros((1, BLK), F32)
            for w in range(SPAN + 1):
                shift = jnp.where(first + w >= 0, top, -NEG) if w < SPAN else top
                e = jnp.exp2(s_ref[w] * EXP_SCALE - shift)
                s_ref[w] = e
                total = total + jnp.sum(e, axis=0, keepdims=True)
                weighted = weighted + jnp.sum(e * dp_ref[w], axis=0, keepdims=True)
            inverse = 1.0 / total
            mean = weighted * inverse
            inverse_scaled = inverse * SCALE
            att = jnp.zeros((HD, BLK), F32)
            dq = jnp.zeros((HD, BLK), F32)
            for w in range(SPAN + 1):
                e = s_ref[w]
                weights = (e * inverse).astype(BF)
                dscore = ((e * inverse_scaled) * (dp_ref[w] - mean)).astype(BF)
                dkv[hl, qi + w, :, :HD] += jnp.dot(dscore, query, preferred_element_type=F32)
                dkv[hl, qi + w, :, HD:] += jnp.dot(weights, grad, preferred_element_type=F32)
                att = att + jnp.dot(kvt[qi + w, HD:, :], weights, preferred_element_type=F32)
                dq = dq + jnp.dot(kvt[qi + w, :HD, :], dscore, preferred_element_type=F32)
            obuf[hl, qi, :, :HD] = att.T.astype(BF)
            obuf[hl, qi, :, HD:] = dq.T.astype(BF)

            @pl.when(qi == me)
            def _():
                o_local(hl, 0).start()
                o_local(hl, 1).start()

            @pl.when(qi != me)
            def _():
                o_send(hl, qi, 0).start()
                o_send(hl, qi, 1).start()

            sbuf[hl, qi] = dkv[hl, qi].astype(BF)
            back(hl, qi, 1).start()

        loop(0, 4, one_block)

        def one_back(i):
            sbuf[hl, 4 + i] = dkv[hl, 4 + i].astype(BF)
            back(hl, i, 0).start()

        loop(0, 4, one_back)

    def finish(hl):
        def one(i):
            back(hl, i, 0).wait_recv()
            back(hl, i, 1).wait_recv()
            whole = dkv[hl, SPAN + i] + rbuf[hl, 0, i].astype(F32) + rbuf[hl, 1, i].astype(F32)
            kvf[hl, i] = whole.astype(BF)

            @pl.when(i == me)
            def _():
                g_local(hl).start()

            @pl.when(i != me)
            def _():
                g_send(hl, i).start()

        loop(0, 4, one)

    x_copy = pltpu.make_async_copy(x_in, xv, xl)
    x_copy.start()
    for hl in range(2):
        for kv in range(2):
            loop(0, 4, lambda j: w_local(hl, j, kv).start())
    greet(
        [(base + (me + r) % 4, dp) for r in range(4) if r]
        + [(base + (me + r) % 4, other) for r in range(4)]
        + [(near_next, dp), (far_next, dp), (near_prev, dp), (far_prev, dp)]
    )

    def w_start(hl):
        def one(j):
            w_send(hl, j, 0).start()
            w_send(hl, j, 1).start()

        loop(0, 4, one)

    def q_start(hl):
        q_local(hl, 0).start()
        q_local(hl, 1).start()

        def one(j):
            q_send(hl, j, 0).start()
            q_send(hl, j, 1).start()

        others(one)

    w_start(0)
    x_copy.wait()
    project(0)
    others(lambda j: kv_send(0, j).wait_send())
    w_start(1)
    q_start(0)
    send_halo(0)
    project(1)
    q_start(1)
    send_halo(1)
    f_local().start()
    loop(1, 8, lambda t: f_send((me + t % 4) % 4, (dp + t // 4) % 2).start())

    def ready(hl):
        def one(i):
            halo(hl, i, 0).wait_recv()
            halo(hl, i, 1).wait_recv()

        loop(0, 4, one)
        q_local(hl, 0).wait()
        q_local(hl, 1).wait()

        def two(j):
            q_arrive(hl, j, 0).wait_recv()
            q_arrive(hl, j, 1).wait_recv()

        others(two)

    ready(0)
    attend(0)
    ready(1)
    attend(1)
    finish(0)
    finish(1)
    kvf_copy = pltpu.make_async_copy(kvf, kvf_out, el.at[0])
    kvf_copy.start()
    for hl in range(2):
        g_local(hl).wait()
        others(lambda j: g_arrive(hl, j).wait_recv())

    def feature(n):
        at = pl.multiple_of(n * 256, 256)
        acc = jnp.zeros((BLK, 256), F32)
        for idx in range(8):
            acc = acc + lax.dot_general(
                kvg[idx], wf[idx, pl.ds(at, 256), :], NT, preferred_element_type=F32
            )
        fgv[:, pl.ds(at, 256)] = acc.astype(BF)

    loop(0, 8, feature)
    fg_copy = pltpu.make_async_copy(fgv, fg_out, el.at[1])
    fg_copy.start()

    for hl in range(2):
        def w_end(j):
            w_send(hl, j, 0).wait_send()
            w_send(hl, j, 1).wait_send()
            w_swap(hl, j, core).wait_send()

        loop(0, 4, w_end)

        def four_end(i):
            for far in range(2):
                halo(hl, i, far).wait_send()
                back(hl, i, far).wait_send()

        loop(0, 4, four_end)

        def three_end(j):
            if hl == 1:
                kv_send(hl, j).wait_send()
            g_send(hl, j).wait_send()
            for which in range(2):
                q_send(hl, j, which).wait_send()
                o_send(hl, j, which).wait_send()
                o_arrive(hl, j, which).wait_recv()

        others(three_end)
        o_local(hl, 0).wait()
        o_local(hl, 1).wait()
    f_local().wait()

    def f_end(t):
        j, d = (me + t % 4) % 4, (dp + t // 4) % 2
        f_send(j, d).wait_send()
        f_arrive(j, d).wait_recv()

    loop(1, 8, f_end)
    kvf_copy.wait()
    fg_copy.wait()


def weight_kernel(
    fall_in, kvf_in, dw_out,
    fv, gv, dwb, r1, dz, r2, s3, r3,
    il, ps, pr, s1s, s1r, s2s, s2r, s3s, s3r,
):
    n_z = lax.axis_size("seq") // 16
    seq, dp, me, base = place()
    xi = (seq // 4) % 4
    zi = seq // 16
    other = 1 - dp

    f_copy = pltpu.make_async_copy(fall_in, fv, il.at[0])
    g_copy = pltpu.make_async_copy(kvf_in, gv.at[dp], il.at[1])
    f_copy.start()
    g_copy.start()
    x_seq = lambda x: zi * 16 + x * 4 + me
    z_seq = lambda z: z * 16 + xi * 4 + me
    greet(
        [(seq, other)]
        + [(base + (me + r) % 4, dp) for r in range(1, 4)]
        + [(x_seq((xi + r) % 4), dp) for r in range(1, 4)]
        + [(z_seq((zi + r) % n_z), dp) for r in range(1, n_z)]
    )
    p_copy = remote(kvf_in, gv.at[dp], ps, pr, seq, other)
    p_copy.start()
    f_copy.wait()
    g_copy.wait()
    remote(kvf_in, gv.at[other], ps, pr, seq, other).wait_recv()

    def tile(t):
        at = pl.multiple_of(t * 256, 256)
        for hl in range(2):
            acc = jnp.zeros((256, 2 * HD), F32)
            for s in range(2):
                for b in range(4):
                    acc = acc + lax.dot_general(
                        fv[s, b, :, pl.ds(at, 256)], gv[s, hl, b], TN, preferred_element_type=F32
                    )
            for zz in range(2):
                for xx in range(4):
                    lo = (zz * 4 + xx) * 32
                    dwb[xx, 2 * t + zz, :, hl * 256:(hl + 1) * 256] = acc[lo:lo + 32].astype(BF)

    loop(0, 4, tile)

    def first(x):
        return remote(dwb.at[x], r1.at[xi], s1s.at[x], s1r.at[xi], x_seq(x), dp)

    def first_arrive(x):
        return remote(dwb.at[x], r1.at[x], s1s.at[x], s1r.at[x], x_seq(x), dp)

    loop(1, 4, lambda r: first((xi + r) % 4).start())
    loop(1, 4, lambda r: first_arrive((xi + r) % 4).wait_recv())

    def second(z):
        return remote(dz.at[z], r2.at[zi], s2s.at[z], s2r.at[zi], z_seq(z), dp)

    def second_arrive(z):
        return remote(dz.at[z], r2.at[z], s2s.at[z], s2r.at[z], z_seq(z), dp)

    def add_x(z):
        acc = dwb[xi, z].astype(F32)
        for r in range(1, 4):
            acc = acc + r1[(xi + r) % 4, z].astype(F32)
        return acc

    def one_z(r):
        z = (zi + r) % n_z
        dz[z] = add_x(z).astype(BF)
        second(z).start()

    loop(1, n_z, one_z)
    acc = add_x(zi)
    loop(1, n_z, lambda r: second_arrive((zi + r) % n_z).wait_recv())
    for r in range(1, n_z):
        acc = acc + r2[(zi + r) % n_z].astype(F32)
    for j in range(4):
        s3[j] = acc[j * 8:(j + 1) * 8]

    def third(j):
        return remote(s3.at[j], r3.at[me], s3s.at[j], s3r.at[me], base + j, dp)

    def third_arrive(j):
        return remote(s3.at[j], r3.at[j], s3s.at[j], s3r.at[j], base + j, dp)

    loop(1, 4, lambda r: third((me + r) % 4).start())
    r3[me] = s3[me]
    loop(1, 4, lambda r: third_arrive((me + r) % 4).wait_recv())
    for j in range(4):
        for hl in range(2):
            for kv in range(2):
                head = kv * 1024 + (2 * j + hl) * HD
                lo = hl * 256 + kv * HD
                dw_out[:, head:head + HD] = r3[j, :, lo:lo + HD]

    p_copy.wait_send()
    loop(1, 4, lambda r: first((xi + r) % 4).wait_send())
    loop(1, n_z, lambda r: second((zi + r) % n_z).wait_send())
    loop(1, 4, lambda r: third((me + r) % 4).wait_send())


def local(features, queries, kv_weight, upstream):
    dma = pltpu.SemaphoreType.DMA
    anywhere = pl.BlockSpec(memory_space=pl.ANY)
    vmem = pl.BlockSpec(memory_space=pltpu.VMEM)
    sds = jax.ShapeDtypeStruct
    att, dq, fg, kvf, fall = pl.pallas_call(
        attention_kernel,
        out_shape=(
            sds((256, 1024), BF), sds((256, 1024), BF), sds((256, 2048), BF),
            sds((2, 4, 256, 256), BF), sds((2, 4, 256, 1024), BF),
        ),
        in_specs=[anywhere] * 4,
        out_specs=(anywhere,) * 5,
        scratch_shapes=[
            pltpu.VMEM((8, 2048, 256), BF),
            pltpu.VMEM((256, 2048), BF),
            pltpu.VMEM((8, 256, 256), BF),
            pltpu.VMEM((2, 12, 256, 256), BF),
            pltpu.VMEM((12, 256, 256), BF),
            pltpu.VMEM((2, 4, 256, 256), BF),
            pltpu.VMEM((9, 256, 256), F32),
            pltpu.VMEM((9, 256, 256), F32),
            pltpu.VMEM((2, 12, 256, 256), F32),
            pltpu.VMEM((2, 8, 256, 256), BF),
            pltpu.VMEM((2, 2, 4, 256, 256), BF),
            pltpu.VMEM((2, 4, 256, 256), BF),
            pltpu.VMEM((8, 256, 256), BF),
            pltpu.VMEM((2, 4, 256, 256), BF),
            pltpu.VMEM((256, 2048), BF),
            dma((8, 2)), dma((8, 2)), dma((8, 2)), dma((8,)), dma((8,)), dma,
            dma((2, 4)), dma((2, 4)), dma((2,)),
            dma((2, 2, 4)), dma((2, 2, 4)),
            dma((2, 4, 2)), dma((2, 4, 2)), dma((2, 2)),
            dma((2, 4)), dma((2, 4)), dma,
            dma((2, 4, 2)), dma((2, 4, 2)), dma((2, 2)),
            dma((2, 2, 4)), dma((2, 2, 4)),
            dma((2, 4)), dma((2, 4)), dma((2,)), dma((2,)),
        ],
        compiler_params=pltpu.CompilerParams(
            collective_id=0, has_side_effects=True, vmem_limit_bytes=56 << 20
        ),
        name="attention",
    )(features[0], queries[0], kv_weight, upstream[0])
    weight_grad = pl.pallas_call(
        weight_kernel,
        out_shape=sds((8, 2048), F32),
        in_specs=[anywhere] * 2,
        out_specs=vmem,
        scratch_shapes=[
            pltpu.VMEM((2, 4, 256, 1024), BF),
            pltpu.VMEM((2, 2, 4, 256, 256), BF),
            pltpu.VMEM((4, 8, 32, 512), BF),
            pltpu.VMEM((4, 8, 32, 512), BF),
            pltpu.VMEM((8, 32, 512), BF),
            pltpu.VMEM((8, 32, 512), BF),
            pltpu.VMEM((4, 8, 512), F32),
            pltpu.VMEM((4, 8, 512), F32),
            dma((2,)), dma, dma,
            dma((4,)), dma((4,)), dma((8,)), dma((8,)), dma((4,)), dma((4,)),
        ],
        compiler_params=pltpu.CompilerParams(
            collective_id=1, has_side_effects=True, vmem_limit_bytes=40 << 20
        ),
        name="weight_gradient",
    )(fall, kvf)
    return (att[None], dq[None], fg[None], weight_grad)


def solution(mesh):
    return jax.shard_map(
        local,
        mesh=mesh,
        in_specs=(P("dp", "seq", None), P("dp", "seq", None), P("dp", None), P("dp", "seq", None)),
        out_specs=(
            P("dp", "seq", None),
            P("dp", "seq", None),
            P("dp", "seq", None),
            P(("dp", "seq"), None),
        ),
        check_vma=False,
    )
```

```python
import math

import jax
import jax.numpy as jnp
from jax import lax
from jax.experimental import pallas as pl
from jax.experimental.pallas import tpu as pltpu
from jax.sharding import PartitionSpec as P

HD = 128
BLK = 256
SPAN = 8
NEG = -1e30
MESH = pl.DeviceIdType.MESH
BF = jnp.bfloat16
F32 = jnp.float32
SCALE = 1.0 / math.sqrt(HD)
EXP_SCALE = SCALE * math.log2(math.e)
NT = (((1,), (1,)), ((), ()))


def loop(lo, hi, body):
    def step(i, carry):
        body(i)
        return carry

    lax.fori_loop(lo, hi, step, 0)


def place():
    seq = lax.axis_index("seq")
    dp = lax.axis_index("dp")
    return seq, dp, seq % 4, seq - seq % 4


def remote(src, dst, send, recv, seq, dp):
    return pltpu.make_async_remote_copy(
        src_ref=src, dst_ref=dst, send_sem=send, recv_sem=recv,
        device_id={"seq": seq, "dp": dp}, device_id_type=MESH,
    )


def greet(partners):
    barrier = pltpu.get_barrier_semaphore()
    for seq, dp in partners:
        pl.semaphore_signal(barrier, inc=1, device_id={"seq": seq, "dp": dp}, device_id_type=MESH)
    pl.semaphore_wait(barrier, len(partners))


def attention_kernel(
    x_in, q_in, w_in, up_in,
    att_out, dq_out, fg_out, dw_out,
    wf, xv, xt, stage, kbuf, kvt, qbuf, s_ref, dp_ref, dkv, sbuf, rbuf, kvf, kvp, kvg, obuf, fgv,
    fv, dwa, dwb, r1, dz, r2, s3, r3,
    wl, ws, wr, wfs, wfr, xl, ks, kr, kl, hs, hr, qs, qr, ql, fs, fr, fl,
    os_, or_, ol, rs, rr, gs, gr, gl, el,
    ps, pr, s1s, s1r, s2s, s2r, s3s, s3r,
):
    n_seq = lax.axis_size("seq")
    n_z = n_seq // 16
    seq, dp, me, base = place()
    xi = (seq // 4) % 4
    zi = seq // 16
    core = seq % 2
    y_hi = (seq // 2) % 2
    other = 1 - dp
    up_y = (y_hi + dp) % 2
    down_y = (y_hi + 1 - dp) % 2
    up_seq = base + up_y * 2 + core
    down_seq = base + down_y * 2 + core
    w_seq = base + ((y_hi + (1 - dp) * (1 - core) + dp * core) % 2) * 2 + core
    pair_seq = base + y_hi * 2 + (1 - core)
    near_next = (seq + 4) % n_seq
    far_next = (seq + 8) % n_seq
    near_prev = (seq + n_seq - 4) % n_seq
    far_prev = (seq + n_seq - 8) % n_seq

    def cols(head_pos, kv):
        return pl.ds(pl.multiple_of(kv * 1024 + head_pos * HD, HD), HD)

    def w_local(hl, j, kv):
        return pltpu.make_async_copy(
            w_in.at[:, cols(2 * j + hl, kv)],
            wf.at[hl * 4 + j, pl.ds(pl.multiple_of(dp * 1024, 1024), 1024), pl.ds(kv * HD, HD)],
            wl.at[hl * 4 + j, kv],
        )

    def w_rows(which_dp, which_core):
        return pl.ds(pl.multiple_of(which_dp * 1024 + which_core * 512, 512), 512)

    def w_send(hl, j, kv):
        return remote(
            w_in.at[pl.ds(pl.multiple_of(core * 512, 512), 512), cols(2 * j + hl, kv)],
            wf.at[hl * 4 + j, w_rows(dp, core), pl.ds(kv * HD, HD)],
            ws.at[hl * 4 + j, kv], wr.at[hl * 4 + j, kv], w_seq, other,
        )

    def w_arrive(hl, j, kv):
        part = wf.at[hl * 4 + j, w_rows(other, core), pl.ds(kv * HD, HD)]
        return remote(part, part, ws.at[hl * 4 + j, kv], wr.at[hl * 4 + j, kv], w_seq, other)

    def w_swap(hl, j, which_core):
        part = wf.at[hl * 4 + j, w_rows(other, which_core), :]
        return remote(part, part, wfs.at[hl * 4 + j], wfr.at[hl * 4 + j], pair_seq, dp)

    def kv_send(hl, j):
        return remote(
            stage.at[hl * 4 + j], kbuf.at[hl, SPAN + me], ks.at[hl, j], kr.at[hl, me], base + j, dp
        )

    def kv_arrive(hl, j):
        return remote(
            stage.at[hl * 4 + j], kbuf.at[hl, SPAN + j], ks.at[hl, j], kr.at[hl, j], base + j, dp
        )

    def kv_local(hl):
        return pltpu.make_async_copy(stage.at[hl * 4 + me], kbuf.at[hl, SPAN + me], kl.at[hl])

    def halo(hl, i, far):
        return remote(
            kbuf.at[hl, SPAN + i], kbuf.at[hl, (1 - far) * 4 + i],
            hs.at[hl, far, i], hr.at[hl, far, i], far_next if far else near_next, dp,
        )

    def q_copy(hl, j, which):
        src = (q_in, up_in)[which].at[:, cols(2 * j + hl, 0)]
        return src, qbuf.at[hl, me, :, pl.ds(which * HD, HD)]

    def q_send(hl, j, which):
        src, dst = q_copy(hl, j, which)
        return remote(src, dst, qs.at[hl, j, which], qr.at[hl, me, which], base + j, dp)

    def q_arrive(hl, j, which):
        src, _ = q_copy(hl, j, which)
        return remote(
            src, qbuf.at[hl, j, :, pl.ds(which * HD, HD)],
            qs.at[hl, j, which], qr.at[hl, j, which], base + j, dp,
        )

    def q_local(hl, which):
        src, dst = q_copy(hl, me, which)
        return pltpu.make_async_copy(src, dst, ql.at[hl, which])

    def x_part(which_dp):
        return xt.at[pl.ds(pl.multiple_of(which_dp * 1024, 1024), 1024), :]

    def f_send(j, d):
        return remote(x_part(d), fv.at[dp, me], fs.at[d, j], fr.at[dp, me], base + j, d)

    def f_arrive(j, d):
        return remote(x_part(d), fv.at[d, j], fs.at[d, j], fr.at[d, j], base + j, d)

    def f_local():
        return pltpu.make_async_copy(x_part(dp), fv.at[dp, me], fl)

    def o_send(hl, j, which):
        out = (att_out, dq_out)[which]
        return remote(
            obuf.at[hl, j, :, pl.ds(which * HD, HD)], out.at[:, cols(2 * me + hl, 0)],
            os_.at[hl, j, which], or_.at[hl, me, which], base + j, dp,
        )

    def o_arrive(hl, j, which):
        out = (att_out, dq_out)[which]
        return remote(
            obuf.at[hl, j, :, pl.ds(which * HD, HD)], out.at[:, cols(2 * j + hl, 0)],
            os_.at[hl, j, which], or_.at[hl, j, which], base + j, dp,
        )

    def o_local(hl, which):
        out = (att_out, dq_out)[which]
        return pltpu.make_async_copy(
            obuf.at[hl, me, :, pl.ds(which * HD, HD)], out.at[:, cols(2 * me + hl, 0)],
            ol.at[hl, which],
        )

    def back(hl, i, far):
        return remote(
            sbuf.at[hl, (1 - far) * 4 + i], rbuf.at[hl, far, i],
            rs.at[hl, far, i], rr.at[hl, far, i], far_prev if far else near_prev, dp,
        )

    def g_send(hl, j):
        return remote(
            kvf.at[hl, j], kvg.at[hl * 4 + me], gs.at[hl, j], gr.at[hl, me], base + j, dp
        )

    def g_arrive(hl, j):
        return remote(
            kvf.at[hl, j], kvg.at[hl * 4 + j], gs.at[hl, j], gr.at[hl, j], base + j, dp
        )

    def g_local(hl):
        return pltpu.make_async_copy(kvf.at[hl, me], kvg.at[hl * 4 + me], gl.at[hl])

    def p_send(hl, i):
        return remote(kvf.at[hl, i], kvp.at[hl, i], ps.at[hl, i], pr.at[hl, i], seq, other)

    def x_seq(x):
        return zi * 16 + x * 4 + me

    def z_seq(z):
        return z * 16 + xi * 4 + me

    def first(hl, x):
        return remote(
            dwb.at[hl, x], r1.at[hl, xi], s1s.at[hl, x], s1r.at[hl, xi], x_seq(x), dp
        )

    def first_arrive(hl, x):
        return remote(dwb.at[hl, x], r1.at[hl, x], s1s.at[hl, x], s1r.at[hl, x], x_seq(x), dp)

    def second(hl, z):
        return remote(
            dz.at[hl, z], r2.at[hl, zi], s2s.at[hl, z], s2r.at[hl, zi], z_seq(z), dp
        )

    def second_arrive(hl, z):
        return remote(dz.at[hl, z], r2.at[hl, z], s2s.at[hl, z], s2r.at[hl, z], z_seq(z), dp)

    def third(j):
        return remote(s3.at[j], r3.at[me], s3s.at[j], s3r.at[me], base + j, dp)

    def third_arrive(j):
        return remote(s3.at[j], r3.at[j], s3s.at[j], s3r.at[j], base + j, dp)

    def others(body):
        loop(1, 4, lambda r: body((me + r) % 4))

    def project(hl):
        def forward(j):
            w_arrive(hl, j, 0).wait_recv()
            w_arrive(hl, j, 1).wait_recv()
            w_swap(hl, j, core).start()

        loop(0, 4, forward)

        def one(r):
            j = (me + r) % 4
            w_local(hl, j, 0).wait()
            w_local(hl, j, 1).wait()
            w_swap(hl, j, 1 - core).wait_recv()
            kv = jnp.dot(xv[...], wf[hl * 4 + j], preferred_element_type=F32)
            stage[hl * 4 + j] = kv.astype(BF)

            @pl.when(r < 4)
            def _():
                kv_send(hl, j).start()

            @pl.when(r == 4)
            def _():
                kv_local(hl).start()

        loop(1, 5, one)

    def send_halo(hl):
        kv_local(hl).wait()

        def go(i):
            halo(hl, i, 0).start()
            halo(hl, i, 1).start()

        go(me)

        def one(i):
            kv_arrive(hl, i).wait_recv()
            go(i)

        others(one)

    def attend(hl):
        rows = lax.broadcasted_iota(jnp.int32, (BLK, BLK), 0)
        columns = lax.broadcasted_iota(jnp.int32, (BLK, BLK), 1)

        def one_block(qi):
            query = qbuf[hl, qi, :, :HD]
            grad = qbuf[hl, qi, :, HD:]
            first = base - SPAN + qi
            top = None
            for w in range(SPAN + 1):
                scores = lax.dot_general(
                    kbuf[hl, qi + w, :, :HD], query, NT, preferred_element_type=F32
                )
                if w == 0:
                    scores = jnp.where(rows > columns, scores, NEG)
                if w == SPAN:
                    scores = jnp.where(rows <= columns, scores, NEG)
                s_ref[w] = scores
                here = jnp.max(scores, axis=0, keepdims=True)
                if w < SPAN:
                    here = jnp.where(first + w >= 0, here, NEG)
                top = here if top is None else jnp.maximum(top, here)
                dp_ref[w] = lax.dot_general(
                    kbuf[hl, qi + w, :, HD:], grad, NT, preferred_element_type=F32
                )
            top = top * EXP_SCALE
            total = jnp.zeros((1, BLK), F32)
            weighted = jnp.zeros((1, BLK), F32)
            for w in range(SPAN + 1):
                shift = jnp.where(first + w >= 0, top, -NEG) if w < SPAN else top
                e = jnp.exp2(s_ref[w] * EXP_SCALE - shift)
                s_ref[w] = e
                total = total + jnp.sum(e, axis=0, keepdims=True)
                weighted = weighted + jnp.sum(e * dp_ref[w], axis=0, keepdims=True)
            inverse = 1.0 / total
            mean = weighted * inverse
            inverse_scaled = inverse * SCALE
            att = jnp.zeros((HD, BLK), F32)
            dq = jnp.zeros((HD, BLK), F32)
            for w in range(SPAN + 1):
                e = s_ref[w]
                weights = (e * inverse).astype(BF)
                dscore = ((e * inverse_scaled) * (dp_ref[w] - mean)).astype(BF)
                dkv[hl, qi + w, :, :HD] += jnp.dot(dscore, query, preferred_element_type=F32)
                dkv[hl, qi + w, :, HD:] += jnp.dot(weights, grad, preferred_element_type=F32)
                att = att + jnp.dot(kvt[hl, qi + w, HD:, :], weights, preferred_element_type=F32)
                dq = dq + jnp.dot(kvt[hl, qi + w, :HD, :], dscore, preferred_element_type=F32)
            obuf[hl, qi, :, :HD] = att.T.astype(BF)
            obuf[hl, qi, :, HD:] = dq.T.astype(BF)

            @pl.when(qi == me)
            def _():
                o_local(hl, 0).start()
                o_local(hl, 1).start()

            @pl.when(qi != me)
            def _():
                o_send(hl, qi, 0).start()
                o_send(hl, qi, 1).start()

            sbuf[hl, qi] = dkv[hl, qi].astype(BF)
            back(hl, qi, 1).start()

        loop(0, 4, one_block)

        def one_back(i):
            sbuf[hl, 4 + i] = dkv[hl, 4 + i].astype(BF)
            back(hl, i, 0).start()

        loop(0, 4, one_back)

    def finish(hl):
        def one(i):
            back(hl, i, 0).wait_recv()
            back(hl, i, 1).wait_recv()
            whole = dkv[hl, SPAN + i] + rbuf[hl, 0, i].astype(F32) + rbuf[hl, 1, i].astype(F32)
            kvf[hl, i] = whole.astype(BF)
            p_send(hl, i).start()

            @pl.when(i == me)
            def _():
                g_local(hl).start()

            @pl.when(i != me)
            def _():
                g_send(hl, i).start()

        loop(0, 4, one)

    def product(hl, t, sample, kv):
        at = pl.multiple_of(t * 256, 256)
        acc = jnp.zeros((256, 2 * HD), F32)
        for b in range(4):
            acc = acc + jnp.dot(
                fv[sample, b, pl.ds(at, 256), :], kv[hl, b], preferred_element_type=F32
            )
        return acc

    def product_own(hl):
        def tile(t):
            dwa[t] = product(hl, t, dp, kvf)

        loop(0, 4, tile)

    def product_other(hl):
        loop(0, 4, lambda i: p_send(hl, i).wait_recv())

        def tile(t):
            acc = dwa[t] + product(hl, t, other, kvp)
            for zz in range(2):
                for xx in range(4):
                    lo = (zz * 4 + xx) * 32
                    dwb[hl, xx, 2 * t + zz] = acc[lo:lo + 32].astype(BF)

        loop(0, 4, tile)
        loop(1, 4, lambda r: first(hl, (xi + r) % 4).start())

    def add_x(hl, z):
        acc = dwb[hl, xi, z].astype(F32)
        for r in range(1, 4):
            acc = acc + r1[hl, (xi + r) % 4, z].astype(F32)
        return acc

    def second_stage(hl):
        loop(1, 4, lambda r: first_arrive(hl, (xi + r) % 4).wait_recv())

        def one(r):
            z = (zi + r) % n_z
            dz[hl, z] = add_x(hl, z).astype(BF)
            second(hl, z).start()

        loop(1, n_z, one)

    def third_stage(hl):
        acc = add_x(hl, zi)
        loop(1, n_z, lambda r: second_arrive(hl, (zi + r) % n_z).wait_recv())
        for r in range(1, n_z):
            acc = acc + r2[hl, (zi + r) % n_z].astype(F32)
        for j in range(4):
            s3[j, :, hl * 256:(hl + 1) * 256] = acc[j * 8:(j + 1) * 8]

    def w_start(hl):
        def one(j):
            w_send(hl, j, 0).start()
            w_send(hl, j, 1).start()

        loop(0, 4, one)

    def q_start(hl):
        q_local(hl, 0).start()
        q_local(hl, 1).start()

        def one(j):
            q_send(hl, j, 0).start()
            q_send(hl, j, 1).start()

        others(one)

    def turn(hl, b):
        dkv[hl, b] = jnp.zeros((BLK, 2 * HD), F32)
        kvt[hl, b] = kbuf[hl, b].T

    def ready(hl):
        loop(SPAN, SPAN + 4, lambda b: turn(hl, b))

        def near(i):
            halo(hl, i, 0).wait_recv()
            turn(hl, 4 + i)

        def far(i):
            halo(hl, i, 1).wait_recv()
            turn(hl, i)

        loop(0, 4, near)
        loop(0, 4, far)
        q_local(hl, 0).wait()
        q_local(hl, 1).wait()

        def two(j):
            q_arrive(hl, j, 0).wait_recv()
            q_arrive(hl, j, 1).wait_recv()

        others(two)

    def feature(n):
        at = pl.multiple_of(n * 256, 256)
        acc = jnp.zeros((BLK, 256), F32)
        for idx in range(8):
            acc = acc + lax.dot_general(
                kvg[idx], wf[idx, pl.ds(at, 256), :], NT, preferred_element_type=F32
            )
        fgv[:, pl.ds(at, 256)] = acc.astype(BF)

    x_copy = pltpu.make_async_copy(x_in, xv, xl)
    x_copy.start()
    for hl in range(2):
        for kv in range(2):
            loop(0, 4, lambda j: w_local(hl, j, kv).start())
    greet(
        [(base + (me + r) % 4, dp) for r in range(1, 4)]
        + [(base + (me + r) % 4, other) for r in range(4)]
        + [(near_next, dp), (far_next, dp), (near_prev, dp), (far_prev, dp)]
        + [(x_seq((xi + r) % 4), dp) for r in range(1, 4)]
        + [(z_seq((zi + r) % n_z), dp) for r in range(1, n_z)]
    )
    w_start(0)
    x_copy.wait()

    def flip(t):
        at = pl.multiple_of(t * 256, 256)
        xt[pl.ds(at, 256), :] = xv[:, pl.ds(at, 256)].T

    loop(0, 8, flip)
    project(0)
    others(lambda j: kv_send(0, j).wait_send())
    w_start(1)
    send_halo(0)
    project(1)
    q_start(0)
    q_start(1)
    send_halo(1)
    f_local().start()
    loop(1, 8, lambda t: f_send((me + t % 4) % 4, (dp + t // 4) % 2).start())
    ready(0)
    attend(0)
    ready(1)
    attend(1)
    finish(0)
    f_local().wait()
    loop(1, 8, lambda t: f_arrive((me + t % 4) % 4, (dp + t // 4) % 2).wait_recv())
    product_own(0)
    finish(1)
    product_other(0)
    product_own(1)
    for hl in range(2):
        g_local(hl).wait()
        others(lambda j: g_arrive(hl, j).wait_recv())
    product_other(1)
    second_stage(0)
    loop(0, 8, feature)
    fg_copy = pltpu.make_async_copy(fgv, fg_out, el)
    fg_copy.start()
    second_stage(1)
    third_stage(0)
    third_stage(1)
    loop(1, 4, lambda r: third((me + r) % 4).start())
    r3[me] = s3[me]
    loop(1, 4, lambda r: third_arrive((me + r) % 4).wait_recv())
    for j in range(4):
        for hl in range(2):
            for kv in range(2):
                head = kv * 1024 + (2 * j + hl) * HD
                lo = hl * 256 + kv * HD
                dw_out[:, head:head + HD] = r3[j, :, lo:lo + HD]

    for hl in range(2):
        def w_end(j):
            w_send(hl, j, 0).wait_send()
            w_send(hl, j, 1).wait_send()
            w_swap(hl, j, core).wait_send()

        loop(0, 4, w_end)

        def four_end(i):
            for far in range(2):
                halo(hl, i, far).wait_send()
                back(hl, i, far).wait_send()
            p_send(hl, i).wait_send()

        loop(0, 4, four_end)

        def three_end(j):
            if hl == 1:
                kv_send(hl, j).wait_send()
            g_send(hl, j).wait_send()
            for which in range(2):
                q_send(hl, j, which).wait_send()
                o_send(hl, j, which).wait_send()
                o_arrive(hl, j, which).wait_recv()

        others(three_end)
        o_local(hl, 0).wait()
        o_local(hl, 1).wait()
        loop(1, 4, lambda r: first(hl, (xi + r) % 4).wait_send())
        loop(1, n_z, lambda r: second(hl, (zi + r) % n_z).wait_send())
    loop(1, 8, lambda t: f_send((me + t % 4) % 4, (dp + t // 4) % 2).wait_send())
    loop(1, 4, lambda r: third((me + r) % 4).wait_send())
    fg_copy.wait()


def local(features, queries, kv_weight, upstream):
    dma = pltpu.SemaphoreType.DMA
    anywhere = pl.BlockSpec(memory_space=pl.ANY)
    sds = jax.ShapeDtypeStruct
    att, dq, fg, dw = pl.pallas_call(
        attention_kernel,
        out_shape=(
            sds((256, 1024), BF), sds((256, 1024), BF), sds((256, 2048), BF), sds((8, 2048), F32),
        ),
        in_specs=[anywhere] * 4,
        out_specs=(anywhere, anywhere, anywhere, pl.BlockSpec(memory_space=pltpu.VMEM)),
        scratch_shapes=[
            pltpu.VMEM((8, 2048, 256), BF),
            pltpu.VMEM((256, 2048), BF),
            pltpu.VMEM((2048, 256), BF),
            pltpu.VMEM((8, 256, 256), BF),
            pltpu.VMEM((2, 12, 256, 256), BF),
            pltpu.VMEM((2, 12, 256, 256), BF),
            pltpu.VMEM((2, 4, 256, 256), BF),
            pltpu.VMEM((9, 256, 256), F32),
            pltpu.VMEM((9, 256, 256), F32),
            pltpu.VMEM((2, 12, 256, 256), F32),
            pltpu.VMEM((2, 8, 256, 256), BF),
            pltpu.VMEM((2, 2, 4, 256, 256), BF),
            pltpu.VMEM((2, 4, 256, 256), BF),
            pltpu.VMEM((2, 4, 256, 256), BF),
            pltpu.VMEM((8, 256, 256), BF),
            pltpu.VMEM((2, 4, 256, 256), BF),
            pltpu.VMEM((256, 2048), BF),
            pltpu.VMEM((2, 4, 1024, 256), BF),
            pltpu.VMEM((4, 256, 256), F32),
            pltpu.VMEM((2, 4, 8, 32, 256), BF),
            pltpu.VMEM((2, 4, 8, 32, 256), BF),
            pltpu.VMEM((2, 8, 32, 256), BF),
            pltpu.VMEM((2, 8, 32, 256), BF),
            pltpu.VMEM((4, 8, 512), F32),
            pltpu.VMEM((4, 8, 512), F32),
            dma((8, 2)), dma((8, 2)), dma((8, 2)), dma((8,)), dma((8,)), dma,
            dma((2, 4)), dma((2, 4)), dma((2,)),
            dma((2, 2, 4)), dma((2, 2, 4)),
            dma((2, 4, 2)), dma((2, 4, 2)), dma((2, 2)),
            dma((2, 4)), dma((2, 4)), dma,
            dma((2, 4, 2)), dma((2, 4, 2)), dma((2, 2)),
            dma((2, 2, 4)), dma((2, 2, 4)),
            dma((2, 4)), dma((2, 4)), dma((2,)), dma,
            dma((2, 4)), dma((2, 4)),
            dma((2, 4)), dma((2, 4)), dma((2, 8)), dma((2, 8)), dma((4,)), dma((4,)),
        ],
        compiler_params=pltpu.CompilerParams(
            collective_id=0, has_side_effects=True, vmem_limit_bytes=58 << 20
        ),
        name="attention",
    )(features[0], queries[0], kv_weight, upstream[0])
    return (att[None], dq[None], fg[None], dw)


def solution(mesh):
    return jax.shard_map(
        local,
        mesh=mesh,
        in_specs=(P("dp", "seq", None), P("dp", "seq", None), P("dp", None), P("dp", "seq", None)),
        out_specs=(
            P("dp", "seq", None),
            P("dp", "seq", None),
            P("dp", "seq", None),
            P(("dp", "seq"), None),
        ),
        check_vma=False,
    )
```

```python
import math

import jax
import jax.numpy as jnp
from jax import lax
from jax.experimental import pallas as pl
from jax.experimental.pallas import tpu as pltpu
from jax.sharding import PartitionSpec as P

HD = 128
BLK = 256
SPAN = 8
NEG = -1e30
MESH = pl.DeviceIdType.MESH
BF = jnp.bfloat16
F32 = jnp.float32
SCALE = 1.0 / math.sqrt(HD)
EXP_SCALE = SCALE * math.log2(math.e)
NT = (((1,), (1,)), ((), ()))


def loop(lo, hi, body):
    def step(i, carry):
        body(i)
        return carry

    lax.fori_loop(lo, hi, step, 0)


def place():
    seq = lax.axis_index("seq")
    dp = lax.axis_index("dp")
    return seq, dp, seq % 4, seq - seq % 4


def remote(src, dst, send, recv, seq, dp):
    return pltpu.make_async_remote_copy(
        src_ref=src, dst_ref=dst, send_sem=send, recv_sem=recv,
        device_id={"seq": seq, "dp": dp}, device_id_type=MESH,
    )


def greet(partners):
    barrier = pltpu.get_barrier_semaphore()
    for seq, dp in partners:
        pl.semaphore_signal(barrier, inc=1, device_id={"seq": seq, "dp": dp}, device_id_type=MESH)
    return lambda: pl.semaphore_wait(barrier, len(partners))


def attention_kernel(
    x_in, q_in, w_in, up_in,
    att_out, dq_out, fg_out, dw_out,
    wf, xv, xt, stage, kbuf, kvt, qbuf, s_ref, dp_ref, dkv, sbuf, rbuf, kvf, kvp, kvg, obuf, fgv,
    fv, dwa, dwb, r1, dz, r2, s3, r3,
    wl, ws, wr, wfs, wfr, xl, ks, kr, kl, hs, hr, qs, qr, ql, fs, fr, fl, fps, fpr,
    os_, or_, ol, rs, rr, gs, gr, gl, el,
    ps, pr, s1s, s1r, s2s, s2r, s3s, s3r,
):
    n_seq = lax.axis_size("seq")
    n_z = n_seq // 16
    seq, dp, me, base = place()
    xi = (seq // 4) % 4
    zi = seq // 16
    core = seq % 2
    y_hi = (seq // 2) % 2
    other = 1 - dp

    def owner(position, which_dp):
        return (position + 2 * which_dp * (position % 2)) % 4

    mine = owner(me, dp)
    twin_seq = base + owner(mine, other)
    w_seq = base + ((y_hi + (1 - dp) * (1 - core) + dp * core) % 2) * 2 + core
    pair_seq = base + y_hi * 2 + (1 - core)
    near_next = (seq + 4) % n_seq
    far_next = (seq + 8) % n_seq
    near_prev = (seq + n_seq - 4) % n_seq
    far_prev = (seq + n_seq - 8) % n_seq

    def cols(head_pos, kv):
        return pl.ds(pl.multiple_of(kv * 1024 + head_pos * HD, HD), HD)

    def w_local(hl, j, kv):
        return pltpu.make_async_copy(
            w_in.at[:, cols(2 * j + hl, kv)],
            wf.at[hl * 4 + j, pl.ds(pl.multiple_of(dp * 1024, 1024), 1024), pl.ds(kv * HD, HD)],
            wl.at[hl * 4 + j, kv],
        )

    def w_rows(which_dp, which_core):
        return pl.ds(pl.multiple_of(which_dp * 1024 + which_core * 512, 512), 512)

    def w_send(hl, j, kv):
        return remote(
            w_in.at[pl.ds(pl.multiple_of(core * 512, 512), 512), cols(2 * j + hl, kv)],
            wf.at[hl * 4 + j, w_rows(dp, core), pl.ds(kv * HD, HD)],
            ws.at[hl * 4 + j, kv], wr.at[hl * 4 + j, kv], w_seq, other,
        )

    def w_arrive(hl, j, kv):
        part = wf.at[hl * 4 + j, w_rows(other, core), pl.ds(kv * HD, HD)]
        return remote(part, part, ws.at[hl * 4 + j, kv], wr.at[hl * 4 + j, kv], w_seq, other)

    def w_swap(hl, j, kv, which_core):
        part = wf.at[hl * 4 + j, w_rows(other, which_core), pl.ds(kv * HD, HD)]
        return remote(part, part, wfs.at[hl * 4 + j, kv], wfr.at[hl * 4 + j, kv], pair_seq, dp)

    def kv_send(hl, kv, j):
        return remote(
            stage.at[kv, hl * 4 + j], kbuf.at[hl, kv, SPAN + me],
            ks.at[hl, kv, j], kr.at[hl, kv, me], base + owner(j, dp), dp,
        )

    def kv_arrive(hl, kv, i):
        return remote(
            stage.at[kv, hl * 4 + i], kbuf.at[hl, kv, SPAN + i],
            ks.at[hl, kv, i], kr.at[hl, kv, i], base + i, dp,
        )

    def kv_local(hl, kv):
        return pltpu.make_async_copy(
            stage.at[kv, hl * 4 + mine], kbuf.at[hl, kv, SPAN + me], kl.at[hl, kv]
        )

    def halo(hl, kv, i, far):
        return remote(
            kbuf.at[hl, kv, SPAN + i], kbuf.at[hl, kv, (1 - far) * 4 + i],
            hs.at[hl, kv, far, i], hr.at[hl, kv, far, i], far_next if far else near_next, dp,
        )

    def q_copy(hl, j, which):
        src = (q_in, up_in)[which].at[:, cols(2 * j + hl, 0)]
        return src, qbuf.at[hl, me, :, pl.ds(which * HD, HD)]

    def q_send(hl, j, which):
        src, dst = q_copy(hl, j, which)
        return remote(
            src, dst, qs.at[hl, j, which], qr.at[hl, me, which], base + owner(j, dp), dp
        )

    def q_arrive(hl, i, which):
        src, _ = q_copy(hl, mine, which)
        return remote(
            src, qbuf.at[hl, i, :, pl.ds(which * HD, HD)],
            qs.at[hl, i, which], qr.at[hl, i, which], base + i, dp,
        )

    def q_local(hl, which):
        src, dst = q_copy(hl, mine, which)
        return pltpu.make_async_copy(src, dst, ql.at[hl, which])

    def x_part(which_dp):
        return xt.at[pl.ds(pl.multiple_of(which_dp * 1024, 1024), 1024), :]

    def chip(t):
        return (y_hi + t % 2) % 2, (dp + t // 2) % 2

    def f_send(t):
        y, d = chip(t)
        return remote(
            x_part(d), fv.at[dp, me], fs.at[d, y], fr.at[dp, y_hi], base + y * 2 + core, d
        )

    def f_arrive(t):
        y, d = chip(t)
        return remote(
            x_part(d), fv.at[d, y * 2 + core], fs.at[d, y], fr.at[d, y], base + y * 2 + core, d
        )

    def f_local():
        return pltpu.make_async_copy(x_part(dp), fv.at[dp, me], fl)

    def f_pass(t, which_core):
        y, d = chip(t)
        part = fv.at[d, y * 2 + which_core]
        return remote(part, part, fps.at[d, y], fpr.at[d, y], pair_seq, dp)

    def o_send(hl, i, which):
        out = (att_out, dq_out)[which]
        return remote(
            obuf.at[hl, i, :, pl.ds(which * HD, HD)], out.at[:, cols(2 * mine + hl, 0)],
            os_.at[hl, i, which], or_.at[hl, mine, which], base + i, dp,
        )

    def o_arrive(hl, j, which):
        out = (att_out, dq_out)[which]
        return remote(
            obuf.at[hl, j, :, pl.ds(which * HD, HD)], out.at[:, cols(2 * j + hl, 0)],
            os_.at[hl, j, which], or_.at[hl, j, which], base + owner(j, dp), dp,
        )

    def o_local(hl, which):
        out = (att_out, dq_out)[which]
        return pltpu.make_async_copy(
            obuf.at[hl, me, :, pl.ds(which * HD, HD)], out.at[:, cols(2 * mine + hl, 0)],
            ol.at[hl, which],
        )

    def back(hl, i, far):
        return remote(
            sbuf.at[hl, (1 - far) * 4 + i], rbuf.at[hl, far, i],
            rs.at[hl, far, i], rr.at[hl, far, i], far_prev if far else near_prev, dp,
        )

    def g_send(hl, i):
        return remote(
            kvf.at[hl, i], kvg.at[hl * 4 + mine], gs.at[hl, i], gr.at[hl, mine], base + i, dp
        )

    def g_arrive(hl, j):
        return remote(
            kvf.at[hl, j], kvg.at[hl * 4 + j], gs.at[hl, j], gr.at[hl, j], base + owner(j, dp), dp
        )

    def g_local(hl):
        return pltpu.make_async_copy(kvf.at[hl, me], kvg.at[hl * 4 + mine], gl.at[hl])

    def p_send(hl, i):
        return remote(
            kvf.at[hl, i], kvp.at[hl, i], ps.at[hl, i], pr.at[hl, i], twin_seq, other
        )

    def x_seq(x):
        return zi * 16 + x * 4 + me

    def z_seq(z):
        return z * 16 + xi * 4 + me

    def first(hl, x):
        return remote(
            dwb.at[hl, x], r1.at[hl, xi], s1s.at[hl, x], s1r.at[hl, xi], x_seq(x), dp
        )

    def first_arrive(hl, x):
        return remote(dwb.at[hl, x], r1.at[hl, x], s1s.at[hl, x], s1r.at[hl, x], x_seq(x), dp)

    def second(hl, z):
        return remote(
            dz.at[hl, z], r2.at[hl, zi], s2s.at[hl, z], s2r.at[hl, zi], z_seq(z), dp
        )

    def second_arrive(hl, z):
        return remote(dz.at[hl, z], r2.at[hl, z], s2s.at[hl, z], s2r.at[hl, z], z_seq(z), dp)

    def third(i):
        return remote(s3.at[i], r3.at[mine], s3s.at[i], s3r.at[mine], base + i, dp)

    def third_arrive(j):
        return remote(s3.at[j], r3.at[j], s3s.at[j], s3r.at[j], base + owner(j, dp), dp)

    def others(body):
        loop(1, 4, lambda r: body((me + r) % 4))

    def owners(body):
        loop(1, 4, lambda r: body((mine + r) % 4))

    def project(hl, kv):
        def forward(j):
            w_arrive(hl, j, kv).wait_recv()
            w_swap(hl, j, kv, core).start()

        loop(0, 4, forward)

        def two(pair):
            halves = []
            for j in (2 * pair, 2 * pair + 1):
                w_local(hl, j, kv).wait()
                w_swap(hl, j, kv, 1 - core).wait_recv()
                halves.append(wf[hl * 4 + j, :, kv * HD:(kv + 1) * HD])
            both = jnp.dot(
                xv[...], jnp.concatenate(halves, axis=1), preferred_element_type=F32
            ).astype(BF)
            for k in range(2):
                stage[kv, hl * 4 + 2 * pair + k] = both[:, k * HD:(k + 1) * HD]

        loop(0, 2, two)
        owners(lambda j: kv_send(hl, kv, j).start())
        kv_local(hl, kv).start()

    def send_halo(hl, kv):
        kv_local(hl, kv).wait()

        def go(i):
            halo(hl, kv, i, 0).start()
            halo(hl, kv, i, 1).start()

        go(me)

        def one(i):
            kv_arrive(hl, kv, i).wait_recv()
            go(i)

        others(one)

    def attend(hl, lo, hi):
        rows = lax.broadcasted_iota(jnp.int32, (BLK, BLK), 0)
        columns = lax.broadcasted_iota(jnp.int32, (BLK, BLK), 1)

        def one_block(qi):
            query = qbuf[hl, qi, :, :HD]
            grad = qbuf[hl, qi, :, HD:]
            first = base - SPAN + qi
            top = None
            for w in range(SPAN + 1):
                scores = lax.dot_general(
                    kbuf[hl, 0, qi + w], query, NT, preferred_element_type=F32
                )
                if w == 0:
                    scores = jnp.where(rows > columns, scores, NEG)
                if w == SPAN:
                    scores = jnp.where(rows <= columns, scores, NEG)
                s_ref[w] = scores
                here = jnp.max(scores, axis=0, keepdims=True)
                if w < SPAN:
                    here = jnp.where(first + w >= 0, here, NEG)
                top = here if top is None else jnp.maximum(top, here)
                dp_ref[w] = lax.dot_general(
                    kbuf[hl, 1, qi + w], grad, NT, preferred_element_type=F32
                )
            top = top * EXP_SCALE
            total = jnp.zeros((1, BLK), F32)
            weighted = jnp.zeros((1, BLK), F32)
            for w in range(SPAN + 1):
                shift = jnp.where(first + w >= 0, top, -NEG) if w < SPAN else top
                e = jnp.exp2(s_ref[w] * EXP_SCALE - shift)
                s_ref[w] = e
                total = total + jnp.sum(e, axis=0, keepdims=True)
                weighted = weighted + jnp.sum(e * dp_ref[w], axis=0, keepdims=True)
            inverse = 1.0 / total
            mean = weighted * inverse
            inverse_scaled = inverse * SCALE
            att = jnp.zeros((HD, BLK), F32)
            dq = jnp.zeros((HD, BLK), F32)
            for w in range(SPAN + 1):
                e = s_ref[w]
                weights = (e * inverse).astype(BF)
                dscore = ((e * inverse_scaled) * (dp_ref[w] - mean)).astype(BF)
                dkv[hl, qi + w, :, :HD] += jnp.dot(dscore, query, preferred_element_type=F32)
                dkv[hl, qi + w, :, HD:] += jnp.dot(weights, grad, preferred_element_type=F32)
                att = att + jnp.dot(kvt[hl, 1, qi + w], weights, preferred_element_type=F32)
                dq = dq + jnp.dot(kvt[hl, 0, qi + w], dscore, preferred_element_type=F32)
            obuf[hl, qi, :, :HD] = att.T.astype(BF)
            obuf[hl, qi, :, HD:] = dq.T.astype(BF)

            @pl.when(qi == me)
            def _():
                o_local(hl, 0).start()
                o_local(hl, 1).start()

            @pl.when(qi != me)
            def _():
                o_send(hl, qi, 0).start()
                o_send(hl, qi, 1).start()

            sbuf[hl, qi] = dkv[hl, qi].astype(BF)
            back(hl, qi, 1).start()

        loop(lo, hi, one_block)
        if hi < 4:
            return

        def one_back(i):
            sbuf[hl, 4 + i] = dkv[hl, 4 + i].astype(BF)
            back(hl, i, 0).start()

        loop(0, 4, one_back)

    def finish(hl):
        def one(i):
            back(hl, i, 0).wait_recv()
            back(hl, i, 1).wait_recv()
            whole = dkv[hl, SPAN + i] + rbuf[hl, 0, i].astype(F32) + rbuf[hl, 1, i].astype(F32)
            kvf[hl, i] = whole.astype(BF)
            p_send(hl, i).start()

            @pl.when(i == me)
            def _():
                g_local(hl).start()

            @pl.when(i != me)
            def _():
                g_send(hl, i).start()

        loop(0, 4, one)

    def product(hl, t, sample, kv):
        at = pl.multiple_of(t * 256, 256)
        acc = jnp.zeros((256, 2 * HD), F32)
        for b in range(4):
            acc = acc + jnp.dot(
                fv[sample, b, pl.ds(at, 256), :], kv[hl, b], preferred_element_type=F32
            )
        return acc

    def product_own(hl):
        def tile(t):
            dwa[t] = product(hl, t, dp, kvf)

        loop(0, 4, tile)

    def product_other(hl):
        loop(0, 4, lambda i: p_send(hl, i).wait_recv())

        def tile(t):
            acc = dwa[t] + product(hl, t, other, kvp)
            for zz in range(2):
                for xx in range(4):
                    lo = (zz * 4 + xx) * 32
                    dwb[hl, xx, 2 * t + zz] = acc[lo:lo + 32].astype(BF)

        loop(0, 4, tile)

    def first_stage(hl):
        loop(1, 4, lambda r: first(hl, (xi + r) % 4).start())

    def add_x(hl, z):
        acc = dwb[hl, xi, z].astype(F32)
        for r in range(1, 4):
            acc = acc + r1[hl, (xi + r) % 4, z].astype(F32)
        return acc

    def second_stage(hl):
        loop(1, 4, lambda r: first_arrive(hl, (xi + r) % 4).wait_recv())

        def one(r):
            z = (zi + r) % n_z
            dz[hl, z] = add_x(hl, z).astype(BF)
            second(hl, z).start()

        loop(1, n_z, one)

    def third_stage(hl):
        acc = add_x(hl, zi)
        loop(1, n_z, lambda r: second_arrive(hl, (zi + r) % n_z).wait_recv())
        for r in range(1, n_z):
            acc = acc + r2[hl, (zi + r) % n_z].astype(F32)
        for j in range(4):
            s3[j, :, hl * 256:(hl + 1) * 256] = acc[j * 8:(j + 1) * 8]

    def w_start(hl, kv):
        loop(0, 4, lambda j: w_send(hl, j, kv).start())

    def q_start(hl):
        q_local(hl, 0).start()
        q_local(hl, 1).start()

        def one(j):
            q_send(hl, j, 0).start()
            q_send(hl, j, 1).start()

        owners(one)

    def ready(hl):
        for kv in range(2):
            def turn(b):
                kvt[hl, kv, b] = kbuf[hl, kv, b].T

            def near(i):
                halo(hl, kv, i, 0).wait_recv()
                turn(4 + i)

            def far(i):
                halo(hl, kv, i, 1).wait_recv()
                turn(i)

            loop(SPAN, SPAN + 4, turn)
            loop(0, 4, near)
            loop(0, 4, far)

        def clear(b):
            dkv[hl, b] = jnp.zeros((BLK, 2 * HD), F32)

        loop(0, 12, clear)
        q_local(hl, 0).wait()
        q_local(hl, 1).wait()

        def two(i):
            q_arrive(hl, i, 0).wait_recv()
            q_arrive(hl, i, 1).wait_recv()

        others(two)

    def feature(n):
        at = pl.multiple_of(n * 256, 256)
        acc = jnp.zeros((BLK, 256), F32)
        for idx in range(8):
            acc = acc + lax.dot_general(
                kvg[idx], wf[idx, pl.ds(at, 256), :], NT, preferred_element_type=F32
            )
        fgv[:, pl.ds(at, 256)] = acc.astype(BF)

    x_copy = pltpu.make_async_copy(x_in, xv, xl)
    x_copy.start()
    for hl in range(2):
        for kv in range(2):
            loop(0, 4, lambda j: w_local(hl, j, kv).start())
    wait_all = greet(
        [(base + (me + r) % 4, dp) for r in range(1, 4)]
        + [(base + (me + r) % 4, other) for r in range(4)]
        + [(near_next, dp), (far_next, dp), (near_prev, dp), (far_prev, dp)]
        + [(x_seq((xi + r) % 4), dp) for r in range(1, 4)]
        + [(z_seq((zi + r) % n_z), dp) for r in range(1, n_z)]
    )
    x_copy.wait()

    def flip(t):
        at = pl.multiple_of(t * 256, 256)
        xt[pl.ds(at, 256), :] = xv[:, pl.ds(at, 256)].T

    loop(0, 8, flip)
    f_local().start()
    wait_all()
    w_start(0, 0)
    project(0, 0)
    w_start(0, 1)
    send_halo(0, 0)
    project(0, 1)
    w_start(1, 0)
    send_halo(0, 1)
    project(1, 0)
    w_start(1, 1)
    q_start(0)
    send_halo(1, 0)
    project(1, 1)
    q_start(1)
    send_halo(1, 1)
    f_local().wait()
    f_pass(0, core).start()
    loop(1, 4, lambda t: f_send(t).start())
    ready(0)
    attend(0, 0, 4)
    ready(1)
    attend(1, 0, 2)
    finish(0)

    def hand_over(t):
        f_arrive(t).wait_recv()
        f_pass(t, core).start()

    loop(1, 4, hand_over)
    attend(1, 2, 4)
    loop(0, 4, lambda t: f_pass(t, 1 - core).wait_recv())
    product_own(0)
    product_other(0)
    finish(1)
    owners(lambda j: g_arrive(0, j).wait_recv())
    first_stage(0)
    product_own(1)
    product_other(1)
    first_stage(1)
    second_stage(0)
    g_local(0).wait()
    g_local(1).wait()
    owners(lambda j: g_arrive(1, j).wait_recv())
    loop(0, 8, feature)
    fg_copy = pltpu.make_async_copy(fgv, fg_out, el)
    fg_copy.start()
    second_stage(1)
    third_stage(0)
    third_stage(1)
    others(lambda i: third(i).start())
    r3[mine] = s3[me]
    owners(lambda j: third_arrive(j).wait_recv())
    for j in range(4):
        for hl in range(2):
            for kv in range(2):
                head = kv * 1024 + (2 * j + hl) * HD
                lo = hl * 256 + kv * HD
                dw_out[:, head:head + HD] = r3[j, :, lo:lo + HD]

    for hl in range(2):
        for kv in range(2):
            def w_end(j):
                w_send(hl, j, kv).wait_send()
                w_swap(hl, j, kv, core).wait_send()

            loop(0, 4, w_end)
            owners(lambda j: kv_send(hl, kv, j).wait_send())

            def halo_end(i):
                halo(hl, kv, i, 0).wait_send()
                halo(hl, kv, i, 1).wait_send()

            loop(0, 4, halo_end)

        def four_end(i):
            for far in range(2):
                back(hl, i, far).wait_send()
            p_send(hl, i).wait_send()

        loop(0, 4, four_end)

        def owners_end(j):
            for which in range(2):
                q_send(hl, j, which).wait_send()
                o_arrive(hl, j, which).wait_recv()

        owners(owners_end)

        def others_end(i):
            g_send(hl, i).wait_send()
            for which in range(2):
                o_send(hl, i, which).wait_send()

        others(others_end)
        o_local(hl, 0).wait()
        o_local(hl, 1).wait()
        loop(1, 4, lambda r: first(hl, (xi + r) % 4).wait_send())
        loop(1, n_z, lambda r: second(hl, (zi + r) % n_z).wait_send())
    loop(1, 4, lambda t: f_send(t).wait_send())
    loop(0, 4, lambda t: f_pass(t, core).wait_send())
    others(lambda i: third(i).wait_send())
    fg_copy.wait()


def local(features, queries, kv_weight, upstream):
    dma = pltpu.SemaphoreType.DMA
    anywhere = pl.BlockSpec(memory_space=pl.ANY)
    sds = jax.ShapeDtypeStruct
    att, dq, fg, dw = pl.pallas_call(
        attention_kernel,
        out_shape=(
            sds((256, 1024), BF), sds((256, 1024), BF), sds((256, 2048), BF), sds((8, 2048), F32),
        ),
        in_specs=[anywhere] * 4,
        out_specs=(anywhere, anywhere, anywhere, pl.BlockSpec(memory_space=pltpu.VMEM)),
        scratch_shapes=[
            pltpu.VMEM((8, 2048, 256), BF),
            pltpu.VMEM((256, 2048), BF),
            pltpu.VMEM((2048, 256), BF),
            pltpu.VMEM((2, 8, 256, 128), BF),
            pltpu.VMEM((2, 2, 12, 256, 128), BF),
            pltpu.VMEM((2, 2, 12, 128, 256), BF),
            pltpu.VMEM((2, 4, 256, 256), BF),
            pltpu.VMEM((9, 256, 256), F32),
            pltpu.VMEM((9, 256, 256), F32),
            pltpu.VMEM((2, 12, 256, 256), F32),
            pltpu.VMEM((2, 8, 256, 256), BF),
            pltpu.VMEM((2, 2, 4, 256, 256), BF),
            pltpu.VMEM((2, 4, 256, 256), BF),
            pltpu.VMEM((2, 4, 256, 256), BF),
            pltpu.VMEM((8, 256, 256), BF),
            pltpu.VMEM((2, 4, 256, 256), BF),
            pltpu.VMEM((256, 2048), BF),
            pltpu.VMEM((2, 4, 1024, 256), BF),
            pltpu.VMEM((4, 256, 256), F32),
            pltpu.VMEM((2, 4, 8, 32, 256), BF),
            pltpu.VMEM((2, 4, 8, 32, 256), BF),
            pltpu.VMEM((2, 8, 32, 256), BF),
            pltpu.VMEM((2, 8, 32, 256), BF),
            pltpu.VMEM((4, 8, 512), F32),
            pltpu.VMEM((4, 8, 512), F32),
            dma((8, 2)), dma((8, 2)), dma((8, 2)), dma((8, 2)), dma((8, 2)), dma,
            dma((2, 2, 4)), dma((2, 2, 4)), dma((2, 2)),
            dma((2, 2, 2, 4)), dma((2, 2, 2, 4)),
            dma((2, 4, 2)), dma((2, 4, 2)), dma((2, 2)),
            dma((2, 2)), dma((2, 2)), dma, dma((2, 2)), dma((2, 2)),
            dma((2, 4, 2)), dma((2, 4, 2)), dma((2, 2)),
            dma((2, 2, 4)), dma((2, 2, 4)),
            dma((2, 4)), dma((2, 4)), dma((2,)), dma,
            dma((2, 4)), dma((2, 4)),
            dma((2, 4)), dma((2, 4)), dma((2, 8)), dma((2, 8)), dma((4,)), dma((4,)),
        ],
        compiler_params=pltpu.CompilerParams(
            collective_id=0, has_side_effects=True, vmem_limit_bytes=58 << 20
        ),
        name="attention",
    )(features[0], queries[0], kv_weight, upstream[0])
    return (att[None], dq[None], fg[None], dw)


def solution(mesh):
    return jax.shard_map(
        local,
        mesh=mesh,
        in_specs=(P("dp", "seq", None), P("dp", "seq", None), P("dp", None), P("dp", "seq", None)),
        out_specs=(
            P("dp", "seq", None),
            P("dp", "seq", None),
            P("dp", "seq", None),
            P(("dp", "seq"), None),
        ),
        check_vma=False,
    )
```

```python
import math

import jax
import jax.numpy as jnp
from jax import lax
from jax.experimental import pallas as pl
from jax.experimental.pallas import tpu as pltpu
from jax.sharding import PartitionSpec as P

HD = 128
BLK = 256
SPAN = 8
NEG = -1e30
MESH = pl.DeviceIdType.MESH
BF = jnp.bfloat16
F32 = jnp.float32
SCALE = 1.0 / math.sqrt(HD)
EXP_SCALE = SCALE * math.log2(math.e)
NT = (((1,), (1,)), ((), ()))


def loop(lo, hi, body):
    def step(i, carry):
        body(i)
        return carry

    lax.fori_loop(lo, hi, step, 0)


def place():
    seq = lax.axis_index("seq")
    dp = lax.axis_index("dp")
    return seq, dp, seq % 4, seq - seq % 4


def remote(src, dst, send, recv, seq, dp):
    return pltpu.make_async_remote_copy(
        src_ref=src, dst_ref=dst, send_sem=send, recv_sem=recv,
        device_id={"seq": seq, "dp": dp}, device_id_type=MESH,
    )


def greet(partners):
    barrier = pltpu.get_barrier_semaphore()
    for seq, dp in partners:
        pl.semaphore_signal(barrier, inc=1, device_id={"seq": seq, "dp": dp}, device_id_type=MESH)
    return lambda: pl.semaphore_wait(barrier, len(partners))


def attention_kernel(
    x_in, q_in, w_in, up_in,
    att_out, dq_out, fg_out, dw_out,
    wf, pacc, xv, xt, stage, kbuf, kvt, qbuf, s_ref, dp_ref, dkv, sbuf, rbuf, kvf, kvp, kvg, obuf, fgv,
    fv, dwa, dwb, r1, dz, r2, s3, r3,
    wl, ws, wr, wfs, wfr, xl, ks, kr, kl, hs, hr, qs, qr, ql, fs, fr, fl, fps, fpr,
    os_, or_, ol, rs, rr, gs, gr, gl, el,
    ps, pr, s1s, s1r, s2s, s2r, s3s, s3r,
):
    n_seq = lax.axis_size("seq")
    n_z = n_seq // 16
    seq, dp, me, base = place()
    xi = (seq // 4) % 4
    zi = seq // 16
    core = seq % 2
    y_hi = (seq // 2) % 2
    other = 1 - dp

    def owner(position, which_dp):
        return (position + 2 * which_dp * (position % 2)) % 4

    mine = owner(me, dp)
    twin_seq = base + owner(mine, other)
    w_seq = base + ((y_hi + (1 - dp) * (1 - core) + dp * core) % 2) * 2 + core
    pair_seq = base + y_hi * 2 + (1 - core)
    next_seq = (seq + 4) % n_seq
    prev_seq = (seq + n_seq - 4) % n_seq

    def cols(head_pos, kv):
        return pl.ds(pl.multiple_of(kv * 1024 + head_pos * HD, HD), HD)

    def w_at(hl, kv, p):
        return (hl * 2 + kv) * 2 + p

    def half(e):
        return pl.ds(e * HD, HD)

    def w_local(hl, kv, p, e):
        return pltpu.make_async_copy(
            w_in.at[:, cols(2 * (2 * p + e) + hl, kv)],
            wf.at[w_at(hl, kv, p), pl.ds(pl.multiple_of(dp * 1024, 1024), 1024), half(e)],
            wl.at[w_at(hl, kv, p), e],
        )

    def w_rows(which_dp, which_core):
        return pl.ds(pl.multiple_of(which_dp * 1024 + which_core * 512, 512), 512)

    def w_send(hl, kv, p, e):
        at = w_at(hl, kv, p)
        return remote(
            w_in.at[pl.ds(pl.multiple_of(core * 512, 512), 512), cols(2 * (2 * p + e) + hl, kv)],
            wf.at[at, w_rows(dp, core), half(e)], ws.at[at, e], wr.at[at, e], w_seq, other,
        )

    def w_arrive(hl, kv, p, e):
        at = w_at(hl, kv, p)
        part = wf.at[at, w_rows(other, core), half(e)]
        return remote(part, part, ws.at[at, e], wr.at[at, e], w_seq, other)

    def w_swap(hl, kv, p, which_core):
        at = w_at(hl, kv, p)
        part = wf.at[at, w_rows(other, which_core), :]
        return remote(part, part, wfs.at[at], wfr.at[at], pair_seq, dp)

    def kv_send(hl, kv, j):
        return remote(
            stage.at[kv, hl * 4 + j], kbuf.at[hl, kv, SPAN + me],
            ks.at[hl, kv, j], kr.at[hl, kv, me], base + owner(j, dp), dp,
        )

    def kv_arrive(hl, kv, i):
        return remote(
            stage.at[kv, hl * 4 + i], kbuf.at[hl, kv, SPAN + i],
            ks.at[hl, kv, i], kr.at[hl, kv, i], base + i, dp,
        )

    def kv_local(hl, kv):
        return pltpu.make_async_copy(
            stage.at[kv, hl * 4 + mine], kbuf.at[hl, kv, SPAN + me], kl.at[hl, kv]
        )

    def halo(hl, kv, i, far):
        return remote(
            kbuf.at[hl, kv, (2 - far) * 4 + i], kbuf.at[hl, kv, (1 - far) * 4 + i],
            hs.at[hl, kv, far, i], hr.at[hl, kv, far, i], next_seq, dp,
        )

    def q_copy(hl, j, which):
        src = (q_in, up_in)[which].at[:, cols(2 * j + hl, 0)]
        return src, qbuf.at[hl, me, :, pl.ds(which * HD, HD)]

    def q_send(hl, j, which):
        src, dst = q_copy(hl, j, which)
        return remote(
            src, dst, qs.at[hl, j, which], qr.at[hl, me, which], base + owner(j, dp), dp
        )

    def q_arrive(hl, i, which):
        src, _ = q_copy(hl, mine, which)
        return remote(
            src, qbuf.at[hl, i, :, pl.ds(which * HD, HD)],
            qs.at[hl, i, which], qr.at[hl, i, which], base + i, dp,
        )

    def q_local(hl, which):
        src, dst = q_copy(hl, mine, which)
        return pltpu.make_async_copy(src, dst, ql.at[hl, which])

    def x_part(which_dp):
        return xt.at[pl.ds(pl.multiple_of(which_dp * 1024, 1024), 1024), :]

    def chip(t):
        return (y_hi + t % 2) % 2, (dp + t // 2) % 2

    def f_send(t):
        y, d = chip(t)
        return remote(
            x_part(d), fv.at[dp, me], fs.at[d, y], fr.at[dp, y_hi], base + y * 2 + core, d
        )

    def f_arrive(t):
        y, d = chip(t)
        return remote(
            x_part(d), fv.at[d, y * 2 + core], fs.at[d, y], fr.at[d, y], base + y * 2 + core, d
        )

    def f_local():
        return pltpu.make_async_copy(x_part(dp), fv.at[dp, me], fl)

    def f_pass(t, which_core):
        y, d = chip(t)
        part = fv.at[d, y * 2 + which_core]
        return remote(part, part, fps.at[d, y], fpr.at[d, y], pair_seq, dp)

    def o_send(hl, i, which):
        out = (att_out, dq_out)[which]
        return remote(
            obuf.at[hl, i, :, pl.ds(which * HD, HD)], out.at[:, cols(2 * mine + hl, 0)],
            os_.at[hl, i, which], or_.at[hl, mine, which], base + i, dp,
        )

    def o_arrive(hl, j, which):
        out = (att_out, dq_out)[which]
        return remote(
            obuf.at[hl, j, :, pl.ds(which * HD, HD)], out.at[:, cols(2 * j + hl, 0)],
            os_.at[hl, j, which], or_.at[hl, j, which], base + owner(j, dp), dp,
        )

    def o_local(hl, which):
        out = (att_out, dq_out)[which]
        return pltpu.make_async_copy(
            obuf.at[hl, me, :, pl.ds(which * HD, HD)], out.at[:, cols(2 * mine + hl, 0)],
            ol.at[hl, which],
        )

    def back(hl, i, far):
        return remote(
            sbuf.at[hl, (1 - far) * 4 + i], rbuf.at[hl, far, i],
            rs.at[hl, far, i], rr.at[hl, far, i], prev_seq, dp,
        )

    def g_slot(hl, kv, j):
        return kvg.at[w_at(hl, kv, j // 2), :, pl.ds(pl.multiple_of(j % 2 * HD, HD), HD)]

    def g_send(hl, i, kv):
        return remote(
            kvf.at[hl, i, :, half(kv)], g_slot(hl, kv, mine),
            gs.at[hl, i, kv], gr.at[hl, mine, kv], base + i, dp,
        )

    def g_arrive(hl, j, kv):
        return remote(
            kvf.at[hl, j, :, half(kv)], g_slot(hl, kv, j),
            gs.at[hl, j, kv], gr.at[hl, j, kv], base + owner(j, dp), dp,
        )

    def g_local(hl, kv):
        return pltpu.make_async_copy(
            kvf.at[hl, me, :, half(kv)], g_slot(hl, kv, mine), gl.at[hl, kv]
        )

    def p_send(hl, i):
        return remote(
            kvf.at[hl, i], kvp.at[hl, i], ps.at[hl, i], pr.at[hl, i], twin_seq, other
        )

    def x_seq(x):
        return zi * 16 + x * 4 + me

    def z_seq(z):
        return z * 16 + xi * 4 + me

    def first(hl, x):
        return remote(
            dwb.at[hl, x], r1.at[hl, xi], s1s.at[hl, x], s1r.at[hl, xi], x_seq(x), dp
        )

    def first_arrive(hl, x):
        return remote(dwb.at[hl, x], r1.at[hl, x], s1s.at[hl, x], s1r.at[hl, x], x_seq(x), dp)

    def second(hl, z):
        return remote(
            dz.at[hl, z], r2.at[hl, zi], s2s.at[hl, z], s2r.at[hl, zi], z_seq(z), dp
        )

    def second_arrive(hl, z):
        return remote(dz.at[hl, z], r2.at[hl, z], s2s.at[hl, z], s2r.at[hl, z], z_seq(z), dp)

    def third(i):
        return remote(s3.at[i], r3.at[mine], s3s.at[i], s3r.at[mine], base + i, dp)

    def third_arrive(j):
        return remote(s3.at[j], r3.at[j], s3s.at[j], s3r.at[j], base + owner(j, dp), dp)

    def others(body):
        loop(1, 4, lambda r: body((me + r) % 4))

    def owners(body):
        loop(1, 4, lambda r: body((mine + r) % 4))

    def x_cols(which_dp):
        return xv[:, pl.ds(pl.multiple_of(which_dp * 1024, 1024), 1024)]

    def w_half(hl, kv, p, which_dp):
        return wf[w_at(hl, kv, p), pl.ds(pl.multiple_of(which_dp * 1024, 1024), 1024), :]

    def project_own(hl, kv):
        def one(p):
            w_local(hl, kv, p, 0).wait()
            w_local(hl, kv, p, 1).wait()
            pacc[w_at(hl, kv, p)] = jnp.dot(
                x_cols(dp), w_half(hl, kv, p, dp), preferred_element_type=F32
            )

        loop(0, 2, one)

    def project(hl, kv, then=None):
        def forward(p):
            w_arrive(hl, kv, p, 0).wait_recv()
            w_arrive(hl, kv, p, 1).wait_recv()
            w_swap(hl, kv, p, core).start()
            if then is not None:
                w_send(*then, p, 0).start()
                w_send(*then, p, 1).start()

        loop(0, 2, forward)

        def one(p):
            w_swap(hl, kv, p, 1 - core).wait_recv()
            both = pacc[w_at(hl, kv, p)] + jnp.dot(
                x_cols(other), w_half(hl, kv, p, other), preferred_element_type=F32
            )
            for e in range(2):
                stage[kv, hl * 4 + 2 * p + e] = both[:, e * HD:(e + 1) * HD].astype(BF)

        loop(0, 2, one)
        owners(lambda j: kv_send(hl, kv, j).start())
        kv_local(hl, kv).start()

    def send_halo(hl, kv):
        kv_local(hl, kv).wait()

        halo(hl, kv, me, 0).start()

        def one(i):
            kv_arrive(hl, kv, i).wait_recv()
            halo(hl, kv, i, 0).start()

        others(one)

    def relay(hl, kv):
        def one(i):
            halo(hl, kv, i, 0).wait_recv()
            halo(hl, kv, i, 1).start()

        loop(1, 5, lambda r: one((me + r - 1) % 4))

    def attend(hl, lo, hi):
        rows = lax.broadcasted_iota(jnp.int32, (BLK, BLK), 0)
        columns = lax.broadcasted_iota(jnp.int32, (BLK, BLK), 1)

        def one_block(qi):
            query = qbuf[hl, qi, :, :HD]
            grad = qbuf[hl, qi, :, HD:]
            first = base - SPAN + qi
            top = None
            for w in range(SPAN + 1):
                scores = lax.dot_general(
                    kbuf[hl, 0, qi + w], query, NT, preferred_element_type=F32
                )
                if w == 0:
                    scores = jnp.where(rows > columns, scores, NEG)
                if w == SPAN:
                    scores = jnp.where(rows <= columns, scores, NEG)
                s_ref[w] = scores
                here = jnp.max(scores, axis=0, keepdims=True)
                if w < SPAN:
                    here = jnp.where(first + w >= 0, here, NEG)
                top = here if top is None else jnp.maximum(top, here)
                dp_ref[w] = lax.dot_general(
                    kbuf[hl, 1, qi + w], grad, NT, preferred_element_type=F32
                )
            top = top * EXP_SCALE
            total = jnp.zeros((1, BLK), F32)
            weighted = jnp.zeros((1, BLK), F32)
            for w in range(SPAN + 1):
                shift = jnp.where(first + w >= 0, top, -NEG) if w < SPAN else top
                e = jnp.exp2(s_ref[w] * EXP_SCALE - shift)
                s_ref[w] = e
                total = total + jnp.sum(e, axis=0, keepdims=True)
                weighted = weighted + jnp.sum(e * dp_ref[w], axis=0, keepdims=True)
            inverse = 1.0 / total
            mean = weighted * inverse
            inverse_scaled = inverse * SCALE
            att = jnp.zeros((HD, BLK), F32)
            dq = jnp.zeros((HD, BLK), F32)
            for w in range(SPAN + 1):
                e = s_ref[w]
                weights = (e * inverse).astype(BF)
                dscore = ((e * inverse_scaled) * (dp_ref[w] - mean)).astype(BF)
                dkv[hl, qi + w, :, :HD] += jnp.dot(dscore, query, preferred_element_type=F32)
                dkv[hl, qi + w, :, HD:] += jnp.dot(weights, grad, preferred_element_type=F32)
                att = att + jnp.dot(kvt[hl, 1, qi + w], weights, preferred_element_type=F32)
                dq = dq + jnp.dot(kvt[hl, 0, qi + w], dscore, preferred_element_type=F32)
            obuf[hl, qi, :, :HD] = att.T.astype(BF)
            obuf[hl, qi, :, HD:] = dq.T.astype(BF)

            @pl.when(qi == me)
            def _():
                o_local(hl, 0).start()
                o_local(hl, 1).start()

            @pl.when(qi != me)
            def _():
                o_send(hl, qi, 0).start()
                o_send(hl, qi, 1).start()

            sbuf[hl, qi] = dkv[hl, qi].astype(BF)
            back(hl, qi, 1).start()

        loop(lo, hi, one_block)
        if hi < 4:
            return

        def one_back(i):
            back(hl, i, 1).wait_recv()
            sbuf[hl, 4 + i] = (dkv[hl, 4 + i] + rbuf[hl, 1, i].astype(F32)).astype(BF)
            back(hl, i, 0).start()

        loop(0, 4, one_back)

    def finish(hl):
        def one(i):
            back(hl, i, 0).wait_recv()
            whole = dkv[hl, SPAN + i] + rbuf[hl, 0, i].astype(F32)
            kvf[hl, i] = whole.astype(BF)
            p_send(hl, i).start()

            @pl.when(i == me)
            def _():
                g_local(hl, 0).start()
                g_local(hl, 1).start()

            @pl.when(i != me)
            def _():
                g_send(hl, i, 0).start()
                g_send(hl, i, 1).start()

        loop(0, 4, one)

    def product(hl, t, sample, kv):
        at = pl.multiple_of(t * 256, 256)
        acc = jnp.zeros((256, 2 * HD), F32)
        for b in range(4):
            acc = acc + jnp.dot(
                fv[sample, b, pl.ds(at, 256), :], kv[hl, b], preferred_element_type=F32
            )
        return acc

    def product_own(hl):
        def tile(t):
            dwa[t] = product(hl, t, dp, kvf)

        loop(0, 4, tile)

    def product_other(hl):
        loop(0, 4, lambda i: p_send(hl, i).wait_recv())

        def tile(t):
            acc = dwa[t] + product(hl, t, other, kvp)
            for zz in range(2):
                for xx in range(4):
                    lo = (zz * 4 + xx) * 32
                    dwb[hl, xx, 2 * t + zz] = acc[lo:lo + 32].astype(BF)

        loop(0, 4, tile)

    def first_stage(hl):
        loop(1, 4, lambda r: first(hl, (xi + r) % 4).start())

    def add_x(hl, z):
        acc = dwb[hl, xi, z].astype(F32)
        for r in range(1, 4):
            acc = acc + r1[hl, (xi + r) % 4, z].astype(F32)
        return acc

    def second_stage(hl):
        loop(1, 4, lambda r: first_arrive(hl, (xi + r) % 4).wait_recv())

        def one(r):
            z = (zi + r) % n_z
            dz[hl, z] = add_x(hl, z).astype(BF)
            second(hl, z).start()

        loop(1, n_z, one)

    def third_stage(hl):
        acc = add_x(hl, zi)
        loop(1, n_z, lambda r: second_arrive(hl, (zi + r) % n_z).wait_recv())
        for r in range(1, n_z):
            acc = acc + r2[hl, (zi + r) % n_z].astype(F32)
        for j in range(4):
            s3[j, :, hl * 256:(hl + 1) * 256] = acc[j * 8:(j + 1) * 8]

    def w_start(hl, kv):
        def one(p):
            w_send(hl, kv, p, 0).start()
            w_send(hl, kv, p, 1).start()

        loop(0, 2, one)

    def q_start(hl):
        q_local(hl, 0).start()
        q_local(hl, 1).start()

        def one(j):
            q_send(hl, j, 0).start()
            q_send(hl, j, 1).start()

        owners(one)

    def ready(hl):
        for kv in range(2):
            def turn(b):
                kvt[hl, kv, b] = kbuf[hl, kv, b].T

            def far(i):
                halo(hl, kv, i, 1).wait_recv()
                turn(i)

            loop(4, SPAN + 4, turn)
            loop(0, 4, far)

        def clear(b):
            dkv[hl, b] = jnp.zeros((BLK, 2 * HD), F32)

        loop(0, 12, clear)
        q_local(hl, 0).wait()
        q_local(hl, 1).wait()

        def two(i):
            q_arrive(hl, i, 0).wait_recv()
            q_arrive(hl, i, 1).wait_recv()

        others(two)

    def feature(n):
        at = pl.multiple_of(n * 256, 256)
        acc = jnp.zeros((BLK, 256), F32)
        for idx in range(8):
            acc = acc + lax.dot_general(
                kvg[idx], wf[idx, pl.ds(at, 256), :], NT, preferred_element_type=F32
            )
        fgv[:, pl.ds(at, 256)] = acc.astype(BF)

    x_copy = pltpu.make_async_copy(x_in, xv, xl)
    x_copy.start()
    for hl in range(2):
        for kv in range(2):
            for e in range(2):
                loop(0, 2, lambda p: w_local(hl, kv, p, e).start())
    wait_all = greet(
        [(base + (me + r) % 4, dp) for r in range(1, 4)]
        + [(base + (me + r) % 4, other) for r in range(4)]
        + [(next_seq, dp), (prev_seq, dp)]
        + [(x_seq((xi + r) % 4), dp) for r in range(1, 4)]
        + [(z_seq((zi + r) % n_z), dp) for r in range(1, n_z)]
    )
    x_copy.wait()

    def flip(t):
        at = pl.multiple_of(t * 256, 256)
        xt[pl.ds(at, 256), :] = xv[:, pl.ds(at, 256)].T

    loop(0, 8, flip)
    f_local().start()
    for hl in range(2):
        for kv in range(2):
            project_own(hl, kv)
    wait_all()
    w_start(0, 0)
    project(0, 0, (0, 1))
    send_halo(0, 0)
    project(0, 1, (1, 0))
    q_start(0)
    relay(0, 0)
    send_halo(0, 1)
    project(1, 0, (1, 1))
    relay(0, 1)
    send_halo(1, 0)
    ready(0)
    attend(0, 0, 1)
    project(1, 1)
    q_start(1)
    relay(1, 0)
    attend(0, 1, 2)
    send_halo(1, 1)
    attend(0, 2, 3)
    relay(1, 1)
    f_local().wait()
    f_pass(0, core).start()
    loop(1, 4, lambda t: f_send(t).start())
    attend(0, 3, 4)
    ready(1)
    attend(1, 0, 2)
    finish(0)
    attend(1, 2, 4)
    finish(1)

    def hand_over(t):
        f_arrive(t).wait_recv()
        f_pass(t, core).start()

    loop(1, 4, hand_over)
    loop(0, 4, lambda t: f_pass(t, 1 - core).wait_recv())
    product_own(0)
    product_other(0)
    first_stage(0)
    product_own(1)
    product_other(1)
    first_stage(1)
    second_stage(0)
    for hl in range(2):
        for kv in range(2):
            g_local(hl, kv).wait()
            owners(lambda j: g_arrive(hl, j, kv).wait_recv())
    loop(0, 8, feature)
    fg_copy = pltpu.make_async_copy(fgv, fg_out, el)
    fg_copy.start()
    second_stage(1)
    third_stage(0)
    third_stage(1)
    others(lambda i: third(i).start())
    r3[mine] = s3[me]
    owners(lambda j: third_arrive(j).wait_recv())
    for j in range(4):
        for hl in range(2):
            for kv in range(2):
                head = kv * 1024 + (2 * j + hl) * HD
                lo = hl * 256 + kv * HD
                dw_out[:, head:head + HD] = r3[j, :, lo:lo + HD]

    for hl in range(2):
        for kv in range(2):
            def w_end(p):
                w_send(hl, kv, p, 0).wait_send()
                w_send(hl, kv, p, 1).wait_send()
                w_swap(hl, kv, p, core).wait_send()

            loop(0, 2, w_end)
            owners(lambda j: kv_send(hl, kv, j).wait_send())

            def halo_end(i):
                halo(hl, kv, i, 0).wait_send()
                halo(hl, kv, i, 1).wait_send()

            loop(0, 4, halo_end)

        def four_end(i):
            for far in range(2):
                back(hl, i, far).wait_send()
            p_send(hl, i).wait_send()

        loop(0, 4, four_end)

        def owners_end(j):
            for which in range(2):
                q_send(hl, j, which).wait_send()
                o_arrive(hl, j, which).wait_recv()

        owners(owners_end)

        def others_end(i):
            for which in range(2):
                g_send(hl, i, which).wait_send()
                o_send(hl, i, which).wait_send()

        others(others_end)
        o_local(hl, 0).wait()
        o_local(hl, 1).wait()
        loop(1, 4, lambda r: first(hl, (xi + r) % 4).wait_send())
        loop(1, n_z, lambda r: second(hl, (zi + r) % n_z).wait_send())
    loop(1, 4, lambda t: f_send(t).wait_send())
    loop(0, 4, lambda t: f_pass(t, core).wait_send())
    others(lambda i: third(i).wait_send())
    fg_copy.wait()


def local(features, queries, kv_weight, upstream):
    dma = pltpu.SemaphoreType.DMA
    anywhere = pl.BlockSpec(memory_space=pl.ANY)
    sds = jax.ShapeDtypeStruct
    att, dq, fg, dw = pl.pallas_call(
        attention_kernel,
        out_shape=(
            sds((256, 1024), BF), sds((256, 1024), BF), sds((256, 2048), BF), sds((8, 2048), F32),
        ),
        in_specs=[anywhere] * 4,
        out_specs=(anywhere, anywhere, anywhere, pl.BlockSpec(memory_space=pltpu.VMEM)),
        scratch_shapes=[
            pltpu.VMEM((8, 2048, 256), BF),
            pltpu.VMEM((8, 256, 256), F32),
            pltpu.VMEM((256, 2048), BF),
            pltpu.VMEM((2048, 256), BF),
            pltpu.VMEM((2, 8, 256, 128), BF),
            pltpu.VMEM((2, 2, 12, 256, 128), BF),
            pltpu.VMEM((2, 2, 12, 128, 256), BF),
            pltpu.VMEM((2, 4, 256, 256), BF),
            pltpu.VMEM((9, 256, 256), F32),
            pltpu.VMEM((9, 256, 256), F32),
            pltpu.VMEM((2, 12, 256, 256), F32),
            pltpu.VMEM((2, 8, 256, 256), BF),
            pltpu.VMEM((2, 2, 4, 256, 256), BF),
            pltpu.VMEM((2, 4, 256, 256), BF),
            pltpu.VMEM((2, 4, 256, 256), BF),
            pltpu.VMEM((8, 256, 256), BF),
            pltpu.VMEM((2, 4, 256, 256), BF),
            pltpu.VMEM((256, 2048), BF),
            pltpu.VMEM((2, 4, 1024, 256), BF),
            pltpu.VMEM((4, 256, 256), F32),
            pltpu.VMEM((2, 4, 8, 32, 256), BF),
            pltpu.VMEM((2, 4, 8, 32, 256), BF),
            pltpu.VMEM((2, 8, 32, 256), BF),
            pltpu.VMEM((2, 8, 32, 256), BF),
            pltpu.VMEM((4, 8, 512), F32),
            pltpu.VMEM((4, 8, 512), F32),
            dma((8, 2)), dma((8, 2)), dma((8, 2)), dma((8,)), dma((8,)), dma,
            dma((2, 2, 4)), dma((2, 2, 4)), dma((2, 2)),
            dma((2, 2, 2, 4)), dma((2, 2, 2, 4)),
            dma((2, 4, 2)), dma((2, 4, 2)), dma((2, 2)),
            dma((2, 2)), dma((2, 2)), dma, dma((2, 2)), dma((2, 2)),
            dma((2, 4, 2)), dma((2, 4, 2)), dma((2, 2)),
            dma((2, 2, 4)), dma((2, 2, 4)),
            dma((2, 4, 2)), dma((2, 4, 2)), dma((2, 2)), dma,
            dma((2, 4)), dma((2, 4)),
            dma((2, 4)), dma((2, 4)), dma((2, 8)), dma((2, 8)), dma((4,)), dma((4,)),
        ],
        compiler_params=pltpu.CompilerParams(
            collective_id=0, has_side_effects=True, vmem_limit_bytes=58 << 20
        ),
        name="attention",
    )(features[0], queries[0], kv_weight, upstream[0])
    return (att[None], dq[None], fg[None], dw)


def solution(mesh):
    return jax.shard_map(
        local,
        mesh=mesh,
        in_specs=(P("dp", "seq", None), P("dp", "seq", None), P("dp", None), P("dp", "seq", None)),
        out_specs=(
            P("dp", "seq", None),
            P("dp", "seq", None),
            P("dp", "seq", None),
            P(("dp", "seq"), None),
        ),
        check_vma=False,
    )
```
